32 devices in a mesh: strip: 8 (over z, y), panel: 4 (over x, core).
Axes of the slice: x: 2, y: 2, z: 4, core: 2. Of those that a mesh axis runs over, the one named last changes fastest.
Arguments:
- h_cond: float32 [32, 256], P('strip', 'panel'), may hold values from 0.3 to 3
- v_cond: float32 [32, 256], P('strip', 'panel'), may hold values from 0.3 to 3
- confidence: float32 [32, 256], P('strip', 'panel'), may hold values from 1.8e-05 to 0.00225
- teacher: float32 [16, 32, 256], P(None, 'strip', 'panel'), may hold values from -6 to 6
- grad_x: float32 [16, 32, 256], P(None, 'strip', 'panel'), may hold values from -4 to 4
- grad_y: float32 [16, 32, 256], P(None, 'strip', 'panel'), may hold values from -4 to 4
Outputs:
- depth: float32 [16, 32, 256], P(None, 'strip', 'panel')
The draws below stay inside these ranges and needn't reach their ends.
All inputs are finite; a program needn't handle non-finite values.
Results may differ from the reference program's by a relative error of at most 0.0003.
Values sent between devices are 32-bit elements; how exact they have to be, the bound alone decides.
A program may use at most 320 MiB of HBM per device.

```python
import math
import jax
import jax.numpy as jnp
from jax import lax

LON = 256
ROWS_DEV = 4
MAPS = 16
ROWS = 32


def smooth_field(key, leading):
    subkeys = jax.random.split(key, 6)
    polarity = (jax.random.randint(subkeys[0], (leading, 3), 0, 2) * 2 - 1).astype(jnp.float32)
    amplitude = jax.random.uniform(subkeys[1], (leading, 3), jnp.float32, 0.5, 1.0) * polarity
    row_freq = jax.random.uniform(subkeys[2], (leading, 3), jnp.float32, 0.3, 1.5)
    col_freq = jax.random.randint(subkeys[3], (leading, 3), 0, 3).astype(jnp.float32)
    row_phase = jax.random.uniform(subkeys[4], (leading, 3), jnp.float32, 0.0, 2.0 * math.pi)
    col_phase = jax.random.uniform(subkeys[5], (leading, 3), jnp.float32, 0.0, 2.0 * math.pi)
    row_pos = jnp.arange(ROWS, dtype=jnp.float32) / ROWS
    col_pos = jnp.arange(LON, dtype=jnp.float32) / LON
    row_wave = jnp.cos(2.0 * math.pi * row_freq[:, :, None] * row_pos[None, None, :] + row_phase[:, :, None])
    col_wave = jnp.cos(2.0 * math.pi * col_freq[:, :, None] * col_pos[None, None, :] + col_phase[:, :, None])
    pattern = jnp.sum(amplitude[:, :, None, None] * row_wave[:, :, :, None] * col_wave[:, :, None, :], axis=1)
    return pattern / jnp.sum(jnp.abs(amplitude), axis=1)[:, None, None]


def draw_confidence(key, part):
    key = jax.random.fold_in(key, 11)
    smooth_key, rough_key = jax.random.split(key)
    smooth = smooth_field(smooth_key, 1)[0]
    rough = jax.random.uniform(rough_key, (ROWS, LON), jnp.float32, -1.0, 1.0)
    return 0.0003 * jnp.exp(1.2 * smooth + 0.8 * rough)


def draw_teacher(key, part):
    key = jax.random.fold_in(key, 23)
    smooth_key, rough_key = jax.random.split(key)
    smooth = smooth_field(smooth_key, MAPS)
    rough = jax.random.truncated_normal(rough_key, -4.0, 4.0, (MAPS, ROWS, LON), jnp.float32)
    return rough + 2.0 * smooth


def block_scale(stream_key, shape, cuts, least, top_value):
    gain = 1.0
    for axis_at, blocks in cuts:
        draws = jax.random.uniform(jax.random.fold_in(jax.random.fold_in(stream_key, 6), axis_at), (blocks,), jnp.float32, least / len(cuts), top_value / len(cuts))
        gain = gain * jnp.repeat(jnp.exp(draws), shape[axis_at] // blocks).reshape((-1,) + (1,) * (len(shape) - 1 - axis_at))
    return gain


def centred(stream_key, shape, spread, bound, cuts=(), held_as=jnp.bfloat16):
    array = spread * jax.random.normal(stream_key, shape, jnp.float32)
    if cuts:
        array = array * block_scale(stream_key, shape, cuts, -0.22, 0.18)
    return jnp.clip(array, -bound, bound).astype(held_as)


def setup_inputs(seed: int = 0) -> dict:
    splits = jax.random.split(jax.random.key(seed), 7)
    return {
        "h_cond": jnp.clip(jnp.exp(math.log(3.0) - 2.3025851 * jax.random.uniform(splits[0], (ROWS, LON), jnp.float32) ** block_scale(splits[0], (ROWS, LON), ((0, 8), (1, 4)), -0.2, 0.2)), 0.3, 3.0),
        "v_cond": jnp.clip(jnp.exp(math.log(3.0) - 2.3025851 * jax.random.uniform(splits[1], (ROWS, LON), jnp.float32) ** block_scale(splits[1], (ROWS, LON), ((0, 8), (1, 4)), -0.2, 0.2)), 0.3, 3.0),
        "confidence": draw_confidence(jax.random.fold_in(splits[6], 71), 0),
        "teacher": draw_teacher(jax.random.fold_in(splits[6], 71), 0),
        "grad_x": centred(splits[4], (MAPS, ROWS, LON), 0.5, 4.0, ((1, 8), (2, 4)), jnp.float32),
        "grad_y": centred(splits[5], (MAPS, ROWS, LON), 0.5, 4.0, ((1, 8), (2, 4)), jnp.float32),
    }


HIGH = lax.Precision.HIGHEST

def product(left, right):
    return jnp.dot(left.astype(jnp.float32), right.astype(jnp.float32), precision=HIGH, preferred_element_type=jnp.float32)

def apply_to(matrix, vectors):
    return product(vectors, matrix.T)

def row_matrix(diag_row, link_row):
    extent = diag_row.shape[0]
    row_ids = lax.broadcasted_iota(jnp.int32, (extent, extent), 0)
    col_ids = lax.broadcasted_iota(jnp.int32, (extent, extent), 1)
    east = col_ids == (row_ids + 1) % extent
    west = row_ids == (col_ids + 1) % extent
    link = jnp.where(east, link_row[:, None], 0.0) + jnp.where(west, link_row[None, :], 0.0)
    return jnp.where(row_ids == col_ids, diag_row[:, None], 0.0) - link

def inverse(matrix):
    factor = jnp.linalg.cholesky(matrix)
    return jax.scipy.linalg.cho_solve((factor, True), jnp.eye(matrix.shape[0], dtype=jnp.float32))

def reference(h_cond, v_cond, confidence, teacher, grad_x, grad_y):
    rows, extent = h_cond.shape
    hypotheses = teacher.shape[0]
    zero_row = jnp.zeros((1, extent), jnp.float32)
    vertical_above = jnp.concatenate([zero_row, v_cond[:-1]], axis=0)
    flux = v_cond[None] * grad_y
    flux_above = jnp.concatenate([jnp.zeros((hypotheses, 1, extent), jnp.float32), flux[:, :-1]], axis=1)
    along = h_cond[None] * grad_x
    loads = confidence[None] * teacher + jnp.roll(along, 1, axis=2) - along + flux_above - flux
    loads = jnp.transpose(loads, (1, 0, 2))
    diagonal = jnp.roll(h_cond, 1, axis=1) + h_cond + vertical_above + v_cond + confidence
    span = ROWS_DEV * 8
    count = rows // span
    diag_b = diagonal.reshape(count, span, extent)
    link_b = h_cond.reshape(count, span, extent)
    above_b = vertical_above.reshape(count, span, extent)
    load_b = loads.reshape(count, span, hypotheses, extent)
    below_b = v_cond.reshape(count, span, extent)

    def advance(state, inputs):
        inverse_prev, load_prev = state
        diag_row, link_row, coupling, load_row = inputs
        pivot = row_matrix(diag_row, link_row) - coupling[:, None] * inverse_prev * coupling[None, :]
        carried = load_row + coupling[None, :] * apply_to(inverse_prev, load_prev)
        inverse_now = inverse(pivot)
        return ((inverse_now, carried), (inverse_now, carried))
    start = (jnp.eye(extent, dtype=jnp.float32), jnp.zeros((hypotheses, extent), jnp.float32))

    def block_pass(state, block_inputs):
        final, _ = lax.scan(advance, state, block_inputs)
        return (final, state)
    _, starts = lax.scan(block_pass, start, (diag_b, link_b, above_b, load_b))

    def block_back(value_below, block_inputs):
        start_state, diag_rows, link_rows, above_rows, load_rows, below_rows = block_inputs
        _, (inverses, carried) = lax.scan(advance, start_state, (diag_rows, link_rows, above_rows, load_rows))

        def back_row(value_next, inputs):
            inverse_row, carried_row, coupling_below = inputs
            value = apply_to(inverse_row, carried_row + coupling_below[None, :] * value_next)
            return (value, value)
        first_value, values = lax.scan(back_row, value_below, (inverses, carried, below_rows), reverse=True)
        return (first_value, values)
    _, depth = lax.scan(block_back, jnp.zeros((hypotheses, extent), jnp.float32), (starts, diag_b, link_b, above_b, load_b, below_b), reverse=True)
    return jnp.transpose(depth.reshape(rows, hypotheses, extent), (1, 0, 2))
```

```python
import functools

import jax
import jax.numpy as jnp
from jax import lax
from jax.experimental import pallas as pl
from jax.experimental.pallas import tpu as pltpu
from jax.sharding import PartitionSpec as P

HIGH = lax.Precision.HIGHEST


def shifted(value, axis, by):
    count = lax.axis_size(axis)
    pairs = [(i, i + by) for i in range(count) if 0 <= i + by < count]
    return lax.ppermute(value, axis, pairs)


def carried_in(value, axis, join, neutral, backward):
    count, mine = (lax.axis_size(axis), lax.axis_index(axis))
    pieces = jax.tree.map(lambda part: lax.all_gather(part, axis), value)
    if backward:
        pieces = jax.tree.map(lambda part: part[::-1], pieces)
        mine = count - 1 - mine
    total = jax.tree.map(
        lambda part, zero: jnp.full_like(part, 0) + jnp.asarray(zero, part.dtype), value, neutral
    )

    def turn(position, total):
        longer = join(total, jax.tree.map(lambda part: part[position], pieces))
        return jax.tree.map(lambda new, old: jnp.where(position < mine, new, old), longer, total)

    return lax.fori_loop(0, count - 1, turn, total)


def product(left, right):
    return jnp.dot(left, right, precision=HIGH, preferred_element_type=jnp.float32)


def apply_to(matrix, vectors):
    return product(vectors, matrix.T)


def row_matrix(diag_row, link_row):
    extent = diag_row.shape[0]
    row_ids = lax.broadcasted_iota(jnp.int32, (extent, extent), 0)
    col_ids = lax.broadcasted_iota(jnp.int32, (extent, extent), 1)
    east = col_ids == (row_ids + 1) % extent
    west = row_ids == (col_ids + 1) % extent
    link = jnp.where(east, link_row[:, None], 0.0) + jnp.where(west, link_row[None, :], 0.0)
    return jnp.where(row_ids == col_ids, diag_row[:, None], 0.0) - link


def inverse(matrix):
    factor = jnp.linalg.cholesky(matrix)
    return jax.scipy.linalg.cho_solve((factor, True), jnp.eye(matrix.shape[0], dtype=jnp.float32))


def load_update(factor, upper, lower):
    vector = jax.scipy.linalg.cho_solve((factor, True), (upper[4] + lower[3]).T)
    return (upper[3] - product(upper[1], vector).T, lower[4] - product(lower[1].T, vector).T)


def merge_whole(upper, lower):
    extent = upper[2].shape[0]
    factor = jnp.linalg.cholesky(upper[2] + lower[0])
    solved = jax.scipy.linalg.cho_solve(
        (factor, True), jnp.concatenate([upper[1].T, lower[1]], axis=1)
    )
    first_cols = solved[:, :extent]
    second_cols = solved[:, extent:]
    first_load, second_load = load_update(factor, upper, lower)
    return (
        upper[0] - product(upper[1], first_cols),
        -product(upper[1], second_cols),
        lower[2] - product(lower[1].T, second_cols),
        first_load,
        second_load,
    )


def merge_flagged(upper, lower):
    merged = merge_whole(upper[:5], lower[:5])
    upper_empty = upper[5] > 0.5
    lower_empty = lower[5] > 0.5
    picked = tuple(
        (
            jnp.where(upper_empty, lower_part, jnp.where(lower_empty, upper_part, merged_part))
            for upper_part, lower_part, merged_part in zip(upper[:5], lower[:5], merged)
        )
    )
    return picked + (upper[5] * lower[5],)


def chain_maps(earlier_map, later_map):
    return (
        product(later_map[0], earlier_map[0]),
        later_map[1] + apply_to(later_map[0], earlier_map[1]),
    )


def substitute(value_below, inputs):
    gain, offset = inputs
    value = offset + apply_to(gain, value_below)
    return (value, value)


def latitude_shards(h_cond, v_cond, confidence, teacher, grad_x, grad_y):
    slice_cols = h_cond.shape[1]
    local_rows = h_cond.shape[0]
    hypotheses = teacher.shape[0]
    edge_rows = jnp.concatenate([v_cond[-1][None], v_cond[-1][None] * grad_y[:, -1]], axis=0)
    above = shifted(edge_rows, "strip", 1)
    packed = jnp.concatenate(
        [
            h_cond,
            v_cond,
            confidence,
            above,
            teacher.reshape(hypotheses * local_rows, slice_cols),
            grad_x.reshape(hypotheses * local_rows, slice_cols),
            grad_y.reshape(hypotheses * local_rows, slice_cols),
        ],
        axis=0,
    )
    whole = lax.all_gather(packed, "panel", axis=1, tiled=True)
    extent = whole.shape[1]
    horizontal = whole[:local_rows]
    vertical = whole[local_rows : 2 * local_rows]
    weights = whole[2 * local_rows : 3 * local_rows]
    vertical_edge = whole[3 * local_rows]
    flux_edge = whole[3 * local_rows + 1 : 3 * local_rows + 1 + hypotheses]
    base = 3 * local_rows + 1 + hypotheses
    stride = hypotheses * local_rows
    targets = whole[base : base + stride].reshape(hypotheses, local_rows, extent)
    slope_x = whole[base + stride : base + 2 * stride].reshape(hypotheses, local_rows, extent)
    slope_y = whole[base + 2 * stride : base + 3 * stride].reshape(hypotheses, local_rows, extent)
    vertical_above = jnp.concatenate([vertical_edge[None], vertical[:-1]], axis=0)
    flux = vertical[None] * slope_y
    flux_above = jnp.concatenate([flux_edge[:, None], flux[:, :-1]], axis=1)
    along = horizontal[None] * slope_x
    loads = weights[None] * targets + jnp.roll(along, 1, axis=2) - along + flux_above - flux
    loads = jnp.transpose(loads, (1, 0, 2))
    diagonal = jnp.roll(horizontal, 1, axis=1) + horizontal + vertical_above + vertical + weights
    blocks = jax.vmap(row_matrix)(diagonal, horizontal)
    zeros_mat = jnp.zeros((extent, extent), jnp.float32)
    zeros_vec = jnp.zeros((hypotheses, extent), jnp.float32)
    identity = jnp.eye(extent, dtype=jnp.float32)
    start = (zeros_mat, -jnp.diag(vertical_above[0]), blocks[0], zeros_vec, loads[0])

    def fold_step(segment, inputs):
        matrix_row, coupling, load_row = inputs
        piece = (zeros_mat, -jnp.diag(coupling), matrix_row, zeros_vec, load_row)
        merged = merge_whole(segment, piece)
        return (merged, None)

    segment, _ = lax.scan(fold_step, start, (blocks[1:], vertical_above[1:], loads[1:]))
    filled = segment + (jnp.zeros((), jnp.float32),)
    blank = (zeros_mat, zeros_mat, identity, zeros_vec, zeros_vec, jnp.ones((), jnp.float32))
    prefix = carried_in(filled, "strip", merge_flagged, blank, False)
    prefix_matrix, prefix_load = (prefix[2], prefix[4])

    def eliminate(state, inputs):
        inverse_prev, load_prev, pivot_prev = state
        matrix_row, coupling, load_row, coupling_below = inputs
        pivot = matrix_row - coupling[:, None] * inverse_prev * coupling[None, :]
        carried = load_row + coupling[None, :] * apply_to(inverse_prev, load_prev)
        inverse_now = inverse(pivot)
        return (
            (inverse_now, carried, pivot),
            (inverse_now * coupling_below[None, :], apply_to(inverse_now, carried)),
        )

    final_state, (gains, offsets) = lax.scan(
        eliminate,
        (inverse(prefix_matrix), prefix_load, identity),
        (blocks, vertical_above, loads, vertical),
    )

    def compose(mapping, inputs):
        gain, offset = inputs
        return ((product(gain, mapping[0]), offset + apply_to(gain, mapping[1])), None)

    (reach, moved), _ = lax.scan(compose, (identity, zeros_vec), (gains, offsets), reverse=True)
    beyond = carried_in((reach, moved), "strip", chain_maps, (identity, zeros_vec), True)
    _, solution = lax.scan(substitute, beyond[1], (gains, offsets), reverse=True)
    solution = jnp.transpose(solution, (1, 0, 2))
    return lax.dynamic_slice_in_dim(solution, lax.axis_index("panel") * slice_cols, slice_cols, 2)


SHARED = 2
MESH = pl.DeviceIdType.MESH


def power_of_two(n):
    return n >= 2 and n & (n - 1) == 0


def tall_enough(shape, maps, strips, panels):
    local_rows, cols = shape
    rows, group = local_rows * strips, strips // SHARED
    if not (power_of_two(strips) and power_of_two(panels) and group >= 2 and cols % group == 0):
        return False
    width = cols // group
    lanes = 4 * rows
    return (
        lanes == 128
        and cols <= lanes
        and local_rows >= 3
        and power_of_two(width)
        and width % 8 == 0
        and maps % 8 == 0
        and 2 * maps <= rows
        and local_rows * (maps + 8) <= 3 * rows
        and local_rows <= 8
    )


def lane_block(shape, rows):
    return lax.broadcasted_iota(jnp.int32, shape, 1) // rows


def eliminate(systems, rows, group):
    lanes, pieces = systems[0].shape[1], rows // 8
    shape = (8, lanes)
    row_ids = lax.broadcasted_iota(jnp.int32, shape, 0)
    state = [[m[8 * v : 8 * v + 8] for v in range(pieces)] for m in systems]

    def updated(part, column, scale, piece, at):
        pivot = part[piece][at : at + 1] * scale
        fresh = [part[v] - column[v] * pivot for v in range(pieces)]
        fresh[piece] = jnp.where(row_ids == at, pivot, fresh[piece])
        return fresh

    for first in range(0, rows, group):
        columns = [
            [
                [jnp.broadcast_to(p[:, rows + first + t : rows + first + t + 1], shape) for p in m]
                for t in range(group)
            ]
            for m in state
        ]
        for t in range(group):
            piece, at = divmod(first + t, 8)
            for b in range(len(state)):
                column = columns[b][t]
                scale = 1.0 / column[piece][at : at + 1]
                state[b] = updated(state[b], column, scale, piece, at)
                for u in range(t + 1, group):
                    columns[b][u] = updated(columns[b][u], column, scale, piece, at)
    return [jnp.concatenate(m, axis=0) for m in state]


def group_for(count, rows):
    return rows // 2 if count == 1 else rows // 4 if count <= 4 else rows // 8


def merge_segments(tops, bottoms, rows):
    pairs = len(tops) // 2
    solved = eliminate(
        [bottoms[2 * i] + tops[2 * i + 1] for i in range(pairs)], rows, group_for(pairs, rows)
    )
    lanes = solved[0].shape[1]
    block = lane_block(solved[0].shape, rows)
    zero = jnp.zeros((rows, lanes), jnp.float32)
    new_tops, new_bottoms = [], []
    for x, west, east in zip(solved, tops[::2], bottoms[1::2]):
        x_top = jnp.where(block == 0, 0.0, jnp.where(block == 1, pltpu.roll(x, rows, 1), x))
        x_bottom = jnp.where(block == 2, 0.0, jnp.where(block == 1, pltpu.roll(x, lanes - rows, 1), x))
        right = jnp.concatenate([x_bottom, zero, x_top, zero], axis=0)
        change = product(jnp.concatenate([west, east], axis=0), right)
        new_tops.append(jnp.where(block == 2, 0.0, west) - change[:rows])
        new_bottoms.append(jnp.where(block == 0, 0.0, east) - change[rows:])
    return solved, new_tops, new_bottoms


def merge_tree(tops, bottoms, rows, keep):
    while len(tops) > 1:
        solved, tops, bottoms = merge_segments(tops, bottoms, rows)
        keep(solved)
    return tops[0], bottoms[0]


def sublanes(value, by):
    rows = value.shape[0]
    if by % rows % 8:
        return pltpu.roll(value, by % rows, 0)
    by = by % rows
    return jnp.concatenate([value[rows - by :], value[: rows - by]], axis=0)


def solve_lines(middles, links, rights, rows):
    span = 1
    state = list(zip(middles, links, rights))
    while span < rows:
        state = [line_step(*s, span) for s in state]
        span *= 2
    return [right / middle for middle, _, right in state]


def line_step(middle, link, right, span):
    inverse_middle = 1.0 / middle
    down = sublanes(link, -span)
    north = link * sublanes(inverse_middle, span)
    south = down * sublanes(inverse_middle, -span)
    return (
        middle - north * link - south * down,
        north * sublanes(link, span),
        right + north * sublanes(right, span) + south * sublanes(right, -span),
    )


def first_merge(fields_ref, width, rows, maps):
    lanes = fields_ref.shape[1]
    shape = (rows, lanes)
    block = lane_block(shape, rows)
    lane = lax.broadcasted_iota(jnp.int32, shape, 1)
    row = lax.broadcasted_iota(jnp.int32, shape, 0)
    diag0, diag1, diag2 = lane == row, lane == row + rows, lane == row + 2 * rows
    upper = jnp.logical_and(lane == row + rows + 1, block == 1)
    lower = jnp.logical_and(lane == row + rows - 1, block == 1)
    load_lane = jnp.logical_and(lane >= 3 * rows, lane < 3 * rows + maps)
    spare = 3 * rows + maps
    east, diagonal, south, north, load = [], [], [], [], []
    for j in range(width):
        f = fields_ref[j * rows : (j + 1) * rows]
        h = jnp.broadcast_to(f[:, spare + 1 : spare + 2], shape)
        v = jnp.broadcast_to(f[:, spare + 2 : spare + 3], shape)
        va = jnp.where(row == 0, 0.0, pltpu.roll(v, 1, 0))
        east.append(h)
        south.append(v)
        north.append(va)
        diagonal.append(jnp.broadcast_to(f[:, spare : spare + 1], shape) + va + h)
        load.append(jnp.where(load_lane, f, 0.0))
    odd = range(1, width, 2)
    solved = solve_lines(
        [diagonal[j] + east[j - 1] for j in odd],
        [north[j] for j in odd],
        [load[j] - jnp.where(diag0, east[j - 1], 0.0) - jnp.where(diag2, east[j], 0.0) for j in odd],
        rows,
    )
    tops, bottoms = [], []
    for j, x in zip(odd, solved):
        x_top = jnp.where(block == 1, pltpu.roll(x, rows, 1), x)
        x_top = jnp.where(block == 0, 0.0, x_top)
        x_bottom = jnp.where(block == 1, pltpu.roll(x, lanes - rows, 1), x)
        x_bottom = jnp.where(block == 2, 0.0, x_bottom)
        tops.append(
            jnp.where(diag1, diagonal[j - 1], 0.0)
            - jnp.where(upper, south[j - 1], 0.0)
            - jnp.where(lower, north[j - 1], 0.0)
            + load[j - 1]
            + east[j - 1] * x_top
        )
        bottoms.append(jnp.where(diag1, east[j], 0.0) + east[j] * x_bottom)
    return solved, tops, bottoms


def looked_up(x, west, east, rows):
    zero = jnp.zeros_like(west)
    right = jnp.concatenate([west, zero, east, zero], axis=0)
    return jnp.where(lane_block(x.shape, rows) == 3, x, 0.0) - product(x, right)


def node_maps(solved, count, rows, lanes):
    lane = lax.broadcasted_iota(jnp.int32, (rows, lanes), 1)
    row = lax.broadcasted_iota(jnp.int32, (rows, lanes), 0)
    maps = {0: jnp.where(lane == row, -1.0, 0.0), count: jnp.where(lane == row + 2 * rows, -1.0, 0.0)}
    step, level, levels = count // 2, 0, []
    position = 0
    while step >= 1:
        levels.append(position)
        position += count // 2 >> level
        level += 1
        step //= 2
    step = count // 2
    for base in reversed(levels):
        for i, node in enumerate(range(step, count, 2 * step)):
            x = solved(base + i)
            if step == count // 2:
                maps[node] = jnp.where(lane_block(x.shape, rows) == 1, 0.0, x)
            else:
                maps[node] = looked_up(x, maps[node - step], maps[node + step], rows)
        step //= 2
    return maps


def compose(maps_in, x, east, rows):
    block = lane_block(maps_in.shape, rows)
    x = jnp.where(lane_block(x.shape, rows) == 1, 0.0, x)
    zero = jnp.zeros_like(x)
    right = jnp.concatenate([jnp.where(east, x, 0.0), zero, jnp.where(east, 0.0, x), zero], axis=0)
    return jnp.where(block == jnp.where(east, 0, 2), 0.0, maps_in) - product(maps_in, right)


def flipped(me, mask):
    bit = 1
    peer = me
    while bit <= mask:
        if mask // bit % 2:
            peer = peer + bit * (1 - 2 * (me // bit % 2))
        bit *= 2
    return peer


def exchange(axis, source, target, send, recv, mask):
    me = lax.axis_index(axis)
    peer = flipped(me, mask)
    copy = pltpu.make_async_remote_copy(
        src_ref=source(peer),
        dst_ref=target(me),
        send_sem=send.at[mask - 1],
        recv_sem=recv.at[mask - 1],
        device_id={axis: peer},
        device_id_type=MESH,
    )
    copy.start()
    return copy


def build_messages(h_ref, v_ref, c_ref, t_ref, gx_ref, gy_ref, stack_ref, rows, maps, width):
    local_rows, cols = h_ref.shape
    lanes = stack_ref.shape[1]
    lane = lax.broadcasted_iota(jnp.int32, (maps, lanes), 1)
    wide = lambda a: jnp.concatenate([a, jnp.zeros((a.shape[0], lanes - cols), jnp.float32)], axis=1)
    h, v, c = wide(h_ref[...]), wide(v_ref[...]), wide(c_ref[...])
    flux_above = jnp.zeros((maps, lanes), jnp.float32)
    edge = jnp.zeros((maps, lanes), jnp.float32)
    stride = maps + 8
    blank = jnp.zeros((5, lanes), jnp.float32)
    for r in range(local_rows):
        rows_r = pl.ds(r, maps, stride=local_rows)
        along = h[r : r + 1] * wide(gx_ref[rows_r, :])
        flux = v[r : r + 1] * wide(gy_ref[rows_r, :])
        west = jnp.where(lane == 0, 0.0, pltpu.roll(along, 1, 1))
        load = c[r : r + 1] * wide(t_ref[rows_r, :]) + west - along + flux_above - flux
        small = jnp.concatenate([v[r : r + 1] + c[r : r + 1], h[r : r + 1], v[r : r + 1], blank], axis=0)
        stack_ref[r * stride : r * stride + maps] = load
        stack_ref[r * stride + maps : (r + 1) * stride] = small
        place = cols - width + r
        moved = pltpu.roll(along, (place - cols + 1) % lanes, 1)
        edge = jnp.where(lane == place, moved, edge)
        flux_above = flux
    base = 3 * rows
    if local_rows * stride < base:
        stack_ref[local_rows * stride : base] = jnp.zeros((base - local_rows * stride, lanes), jnp.float32)
    stack_ref[base : base + maps] = flux_above
    stack_ref[base + maps : base + 2 * maps] = edge
    if base + 2 * maps < lanes:
        stack_ref[base + 2 * maps :] = jnp.zeros((lanes - base - 2 * maps, lanes), jnp.float32)
    return stack_ref[...].T


def spread_fields(got_ref, fields_ref, edge_ref, rows, maps, width):
    strips, _, lanes = got_ref.shape
    local_rows = rows // strips
    stride, base = maps + 8, 3 * rows
    shape = (width, lanes)
    lane = lax.broadcasted_iota(jnp.int32, shape, 1)
    load_lane = jnp.logical_and(lane >= base, lane < base + maps)
    for s in range(strips):
        part = got_ref[s]
        for r in range(local_rows):
            moved = pltpu.roll(part, (base - r * stride) % lanes, 1)
            if r == 0 and s > 0:
                moved = moved + jnp.where(load_lane, got_ref[s - 1], 0.0)
            for j in range(0, width, 8):
                fields_ref[pl.ds(j * rows + s * local_rows + r, 8, stride=rows), :] = moved[j : j + 8]
        edge_ref[s * local_rows : (s + 1) * local_rows] = pltpu.roll(part, lanes - maps, 1)[:local_rows]


def solve_kernel(
    h_in, v_in, c_in, t_in, gx_in, gy_in, out_ref,
    h_ref, v_ref, c_ref, t_ref, gx_ref, gy_ref, stack_ref, parts_ref, got_ref, fields_ref, edge_ref,
    local_ref, nodes_ref, near_ref, maps_ref, got_maps_ref, pans_ref, path_ref,
    load_sem, send_in, recv_in, send_near, recv_near, send_maps, recv_maps, send_pan, recv_pan,
    *, rows, maps,
):
    strips, me = lax.axis_size("strip"), lax.axis_index("strip")
    panels, panel = lax.axis_size("panel"), lax.axis_index("panel")
    group, width, lanes = parts_ref.shape
    local_rows = rows // strips
    cols = group * width
    barrier = pltpu.get_barrier_semaphore()
    far_first = list(range(strips - 1, 0, -1))
    for mask in far_first:
        pl.semaphore_signal(barrier, inc=1, device_id={"strip": flipped(me, mask)}, device_id_type=MESH)
    for mask in range(1, panels):
        pl.semaphore_signal(barrier, inc=1, device_id={"panel": flipped(panel, mask)}, device_id_type=MESH)
    pairs = zip((h_in, v_in, c_in, t_in, gx_in, gy_in), (h_ref, v_ref, c_ref, t_ref, gx_ref, gy_ref))
    loads = [pltpu.make_async_copy(a, b, load_sem.at[i]) for i, (a, b) in enumerate(pairs)]
    for copy in loads:
        copy.start()
    for copy in loads:
        copy.wait()
    turned = build_messages(h_ref, v_ref, c_ref, t_ref, gx_ref, gy_ref, stack_ref, rows, maps, width)
    for g in range(group):
        parts_ref[g] = turned[g * width : (g + 1) * width]
    pl.semaphore_wait(barrier, strips - 1 + panels - 1)

    first = [
        exchange("strip", lambda p: parts_ref.at[p % group], lambda m: got_ref.at[m], send_in, recv_in, mask)
        for mask in far_first
    ]
    mine = me % group
    got_ref[me] = parts_ref[mine]
    for copy in reversed(first):
        copy.wait_recv()
    spread_fields(got_ref, fields_ref, edge_ref, rows, maps, width)
    solved, tops, bottoms = first_merge(fields_ref, width, rows, maps)
    kept = [0]

    def keep(xs):
        for x in xs:
            local_ref[kept[0]] = x
            kept[0] += 1

    keep(solved)
    lane = lax.broadcasted_iota(jnp.int32, (rows, lanes), 1)
    load_lane = jnp.logical_and(lane >= 3 * rows, lane < 3 * rows + maps)
    last_edge = jnp.logical_and(load_lane, mine == group - 1)
    bottoms[-1] = bottoms[-1] + jnp.where(last_edge, edge_ref[...], 0.0)
    top, bottom = merge_tree(tops, bottoms, rows, keep)
    near_ref[mine, :rows] = top
    near_ref[mine, rows:] = bottom
    near = [
        exchange("strip", lambda p: near_ref.at[mine], lambda m: near_ref.at[m % group], send_near, recv_near, mask)
        for mask in range(group - 1, 0, -1)
    ]

    columns = node_maps(lambda i: local_ref[i], width, rows, lanes)
    start = pl.multiple_of((me - mine) * local_rows, group * local_rows)
    for j in range(width):
        nodes_ref[j] = columns[j]
    for j in range(width):
        picked = nodes_ref[j, pl.ds(start, group * local_rows)]
        maps_ref[pl.ds(j, group * local_rows, stride=width), :] = picked
    size = width * local_rows
    spans = lambda p: maps_ref.at[pl.ds(pl.multiple_of(p % group * size, size), size)]
    moved = [
        exchange("strip", spans, lambda m: got_maps_ref.at[m % group], send_maps, recv_maps, mask)
        for mask in range(group - 1, 0, -1)
    ]
    got_maps_ref[mine] = maps_ref[pl.ds(pl.multiple_of(mine * size, size), size)]

    for copy in near:
        copy.wait_recv()
    tops = [near_ref[g, :rows] for g in range(group)]
    bottoms = [near_ref[g, rows:] for g in range(group)]
    inner = []
    top, bottom = merge_tree(tops, bottoms, rows, inner.extend)
    pans_ref[panel, :rows] = top
    pans_ref[panel, rows:] = bottom
    across = [
        exchange("panel", lambda p: pans_ref.at[panel], lambda m: pans_ref.at[m], send_pan, recv_pan, mask)
        for mask in range(1, panels)
    ]
    ends = node_maps(lambda i: inner[i], group, rows, lanes)
    for copy in moved:
        copy.wait_recv()
    for g in range(group):
        part = looked_up(got_maps_ref[g], ends[g], ends[g + 1], rows)
        for r in range(local_rows):
            path_ref[r * cols + g * width : r * cols + (g + 1) * width] = part[r * width : (r + 1) * width]
    for copy in across:
        copy.wait_recv()
    tops = [pans_ref[p, :rows] for p in range(panels)]
    bottoms = [pans_ref[p, rows:] for p in range(panels)]
    path, spot = path_ref[...], panel
    while len(tops) > 1:
        solved, tops, bottoms = merge_segments(tops, bottoms, rows)
        chosen = solved[0]
        for i in range(1, len(solved)):
            chosen = jnp.where(spot // 2 == i, solved[i], chosen)
        path = compose(path, chosen, spot % 2 == 1, rows)
        spot = spot // 2
    top, bottom = tops[0], bottoms[0]
    block = lane_block((rows, lanes), rows)
    wrap = pltpu.roll(top, lanes - rows, 1) + pltpu.roll(bottom, rows, 1)
    closing = top + bottom + jnp.where(block == 1, wrap, 0.0)
    final = eliminate([closing], rows, rows // 2)[0]
    turned = path.T
    weight = turned[:rows] + turned[2 * rows : 3 * rows]
    values = final.T[3 * rows : 3 * rows + maps]
    result = turned[3 * rows : 3 * rows + maps] - product(values, weight)
    for r in range(local_rows):
        out_ref[pl.ds(r, maps, stride=local_rows), :] = result[:, r * cols : (r + 1) * cols]
    for copy in first + near + moved + across:
        copy.wait_send()


def longitude_shards(h_cond, v_cond, confidence, teacher, grad_x, grad_y):
    local_rows, cols = h_cond.shape
    maps = teacher.shape[0]
    strips, panels = lax.axis_size("strip"), lax.axis_size("panel")
    rows, lanes = local_rows * strips, 4 * local_rows * strips
    group = strips // SHARED
    width = cols // group
    f32 = jnp.float32
    dma = pltpu.SemaphoreType.DMA
    flat = (maps * local_rows, cols)
    size = width * local_rows
    values = pl.pallas_call(
        functools.partial(solve_kernel, rows=rows, maps=maps),
        out_shape=jax.ShapeDtypeStruct(flat, f32),
        in_specs=[pl.BlockSpec(memory_space=pl.ANY)] * 6,
        out_specs=pl.BlockSpec(memory_space=pltpu.VMEM),
        scratch_shapes=[
            pltpu.VMEM((local_rows, cols), f32),
            pltpu.VMEM((local_rows, cols), f32),
            pltpu.VMEM((local_rows, cols), f32),
            pltpu.VMEM(flat, f32),
            pltpu.VMEM(flat, f32),
            pltpu.VMEM(flat, f32),
            pltpu.VMEM((lanes, lanes), f32),
            pltpu.VMEM((group, width, lanes), f32),
            pltpu.VMEM((strips, width, lanes), f32),
            pltpu.VMEM((width * rows, lanes), f32),
            pltpu.VMEM((rows, lanes), f32),
            pltpu.VMEM((width - 1, rows, lanes), f32),
            pltpu.VMEM((width, rows, lanes), f32),
            pltpu.VMEM((group, 2 * rows, lanes), f32),
            pltpu.VMEM((group * size, lanes), f32),
            pltpu.VMEM((group, size, lanes), f32),
            pltpu.VMEM((panels, 2 * rows, lanes), f32),
            pltpu.VMEM((local_rows * cols, lanes), f32),
            dma((6,)),
            dma((strips - 1,)),
            dma((strips - 1,)),
            dma((group - 1,)),
            dma((group - 1,)),
            dma((group - 1,)),
            dma((group - 1,)),
            dma((panels - 1,)),
            dma((panels - 1,)),
        ],
        compiler_params=pltpu.CompilerParams(collective_id=0, has_side_effects=True),
    )(h_cond, v_cond, confidence, *(a.reshape(flat) for a in (teacher, grad_x, grad_y)))
    return values.reshape(maps, local_rows, cols)


def shards(h_cond, v_cond, confidence, teacher, grad_x, grad_y):
    strips, panels = lax.axis_size("strip"), lax.axis_size("panel")
    fits = tall_enough(h_cond.shape, teacher.shape[0], strips, panels)
    body = longitude_shards if fits else latitude_shards
    return body(h_cond, v_cond, confidence, teacher, grad_x, grad_y)


def solution(mesh):
    in_specs = (
        P("strip", "panel"),
        P("strip", "panel"),
        P("strip", "panel"),
        P(None, "strip", "panel"),
        P(None, "strip", "panel"),
        P(None, "strip", "panel"),
    )
    out_specs = P(None, "strip", "panel")
    return jax.shard_map(shards, mesh=mesh, in_specs=in_specs, out_specs=out_specs, check_vma=False)
```

```python
import functools

import jax
import jax.numpy as jnp
from jax import lax
from jax.experimental import pallas as pl
from jax.experimental.pallas import tpu as pltpu
from jax.sharding import PartitionSpec as P

HIGH = lax.Precision.HIGHEST


def shifted(value, axis, by):
    count = lax.axis_size(axis)
    pairs = [(i, i + by) for i in range(count) if 0 <= i + by < count]
    return lax.ppermute(value, axis, pairs)


def carried_in(value, axis, join, neutral, backward):
    count, mine = (lax.axis_size(axis), lax.axis_index(axis))
    pieces = jax.tree.map(lambda part: lax.all_gather(part, axis), value)
    if backward:
        pieces = jax.tree.map(lambda part: part[::-1], pieces)
        mine = count - 1 - mine
    total = jax.tree.map(
        lambda part, zero: jnp.full_like(part, 0) + jnp.asarray(zero, part.dtype), value, neutral
    )

    def turn(position, total):
        longer = join(total, jax.tree.map(lambda part: part[position], pieces))
        return jax.tree.map(lambda new, old: jnp.where(position < mine, new, old), longer, total)

    return lax.fori_loop(0, count - 1, turn, total)


def product(left, right):
    return jnp.dot(left, right, precision=HIGH, preferred_element_type=jnp.float32)


def apply_to(matrix, vectors):
    return product(vectors, matrix.T)


def row_matrix(diag_row, link_row):
    extent = diag_row.shape[0]
    row_ids = lax.broadcasted_iota(jnp.int32, (extent, extent), 0)
    col_ids = lax.broadcasted_iota(jnp.int32, (extent, extent), 1)
    east = col_ids == (row_ids + 1) % extent
    west = row_ids == (col_ids + 1) % extent
    link = jnp.where(east, link_row[:, None], 0.0) + jnp.where(west, link_row[None, :], 0.0)
    return jnp.where(row_ids == col_ids, diag_row[:, None], 0.0) - link


def inverse(matrix):
    factor = jnp.linalg.cholesky(matrix)
    return jax.scipy.linalg.cho_solve((factor, True), jnp.eye(matrix.shape[0], dtype=jnp.float32))


def load_update(factor, upper, lower):
    vector = jax.scipy.linalg.cho_solve((factor, True), (upper[4] + lower[3]).T)
    return (upper[3] - product(upper[1], vector).T, lower[4] - product(lower[1].T, vector).T)


def merge_whole(upper, lower):
    extent = upper[2].shape[0]
    factor = jnp.linalg.cholesky(upper[2] + lower[0])
    solved = jax.scipy.linalg.cho_solve(
        (factor, True), jnp.concatenate([upper[1].T, lower[1]], axis=1)
    )
    first_cols = solved[:, :extent]
    second_cols = solved[:, extent:]
    first_load, second_load = load_update(factor, upper, lower)
    return (
        upper[0] - product(upper[1], first_cols),
        -product(upper[1], second_cols),
        lower[2] - product(lower[1].T, second_cols),
        first_load,
        second_load,
    )


def merge_flagged(upper, lower):
    merged = merge_whole(upper[:5], lower[:5])
    upper_empty = upper[5] > 0.5
    lower_empty = lower[5] > 0.5
    picked = tuple(
        (
            jnp.where(upper_empty, lower_part, jnp.where(lower_empty, upper_part, merged_part))
            for upper_part, lower_part, merged_part in zip(upper[:5], lower[:5], merged)
        )
    )
    return picked + (upper[5] * lower[5],)


def chain_maps(earlier_map, later_map):
    return (
        product(later_map[0], earlier_map[0]),
        later_map[1] + apply_to(later_map[0], earlier_map[1]),
    )


def substitute(value_below, inputs):
    gain, offset = inputs
    value = offset + apply_to(gain, value_below)
    return (value, value)


def latitude_shards(h_cond, v_cond, confidence, teacher, grad_x, grad_y):
    slice_cols = h_cond.shape[1]
    local_rows = h_cond.shape[0]
    hypotheses = teacher.shape[0]
    edge_rows = jnp.concatenate([v_cond[-1][None], v_cond[-1][None] * grad_y[:, -1]], axis=0)
    above = shifted(edge_rows, "strip", 1)
    packed = jnp.concatenate(
        [
            h_cond,
            v_cond,
            confidence,
            above,
            teacher.reshape(hypotheses * local_rows, slice_cols),
            grad_x.reshape(hypotheses * local_rows, slice_cols),
            grad_y.reshape(hypotheses * local_rows, slice_cols),
        ],
        axis=0,
    )
    whole = lax.all_gather(packed, "panel", axis=1, tiled=True)
    extent = whole.shape[1]
    horizontal = whole[:local_rows]
    vertical = whole[local_rows : 2 * local_rows]
    weights = whole[2 * local_rows : 3 * local_rows]
    vertical_edge = whole[3 * local_rows]
    flux_edge = whole[3 * local_rows + 1 : 3 * local_rows + 1 + hypotheses]
    base = 3 * local_rows + 1 + hypotheses
    stride = hypotheses * local_rows
    targets = whole[base : base + stride].reshape(hypotheses, local_rows, extent)
    slope_x = whole[base + stride : base + 2 * stride].reshape(hypotheses, local_rows, extent)
    slope_y = whole[base + 2 * stride : base + 3 * stride].reshape(hypotheses, local_rows, extent)
    vertical_above = jnp.concatenate([vertical_edge[None], vertical[:-1]], axis=0)
    flux = vertical[None] * slope_y
    flux_above = jnp.concatenate([flux_edge[:, None], flux[:, :-1]], axis=1)
    along = horizontal[None] * slope_x
    loads = weights[None] * targets + jnp.roll(along, 1, axis=2) - along + flux_above - flux
    loads = jnp.transpose(loads, (1, 0, 2))
    diagonal = jnp.roll(horizontal, 1, axis=1) + horizontal + vertical_above + vertical + weights
    blocks = jax.vmap(row_matrix)(diagonal, horizontal)
    zeros_mat = jnp.zeros((extent, extent), jnp.float32)
    zeros_vec = jnp.zeros((hypotheses, extent), jnp.float32)
    identity = jnp.eye(extent, dtype=jnp.float32)
    start = (zeros_mat, -jnp.diag(vertical_above[0]), blocks[0], zeros_vec, loads[0])

    def fold_step(segment, inputs):
        matrix_row, coupling, load_row = inputs
        piece = (zeros_mat, -jnp.diag(coupling), matrix_row, zeros_vec, load_row)
        merged = merge_whole(segment, piece)
        return (merged, None)

    segment, _ = lax.scan(fold_step, start, (blocks[1:], vertical_above[1:], loads[1:]))
    filled = segment + (jnp.zeros((), jnp.float32),)
    blank = (zeros_mat, zeros_mat, identity, zeros_vec, zeros_vec, jnp.ones((), jnp.float32))
    prefix = carried_in(filled, "strip", merge_flagged, blank, False)
    prefix_matrix, prefix_load = (prefix[2], prefix[4])

    def eliminate(state, inputs):
        inverse_prev, load_prev, pivot_prev = state
        matrix_row, coupling, load_row, coupling_below = inputs
        pivot = matrix_row - coupling[:, None] * inverse_prev * coupling[None, :]
        carried = load_row + coupling[None, :] * apply_to(inverse_prev, load_prev)
        inverse_now = inverse(pivot)
        return (
            (inverse_now, carried, pivot),
            (inverse_now * coupling_below[None, :], apply_to(inverse_now, carried)),
        )

    final_state, (gains, offsets) = lax.scan(
        eliminate,
        (inverse(prefix_matrix), prefix_load, identity),
        (blocks, vertical_above, loads, vertical),
    )

    def compose(mapping, inputs):
        gain, offset = inputs
        return ((product(gain, mapping[0]), offset + apply_to(gain, mapping[1])), None)

    (reach, moved), _ = lax.scan(compose, (identity, zeros_vec), (gains, offsets), reverse=True)
    beyond = carried_in((reach, moved), "strip", chain_maps, (identity, zeros_vec), True)
    _, solution = lax.scan(substitute, beyond[1], (gains, offsets), reverse=True)
    solution = jnp.transpose(solution, (1, 0, 2))
    return lax.dynamic_slice_in_dim(solution, lax.axis_index("panel") * slice_cols, slice_cols, 2)


SHARED = 2
MESH = pl.DeviceIdType.MESH


def power_of_two(n):
    return n >= 2 and n & (n - 1) == 0


def tall_enough(shape, maps, strips, panels):
    local_rows, cols = shape
    rows, group = local_rows * strips, strips // SHARED
    if not (power_of_two(strips) and power_of_two(panels) and group >= 2 and cols % group == 0):
        return False
    width = cols // group
    lanes = 4 * rows
    return (
        lanes == 128
        and cols <= lanes
        and local_rows >= 3
        and power_of_two(width)
        and width % 8 == 0
        and maps % 8 == 0
        and 2 * maps <= rows
        and local_rows * (maps + 8) <= 3 * rows
        and local_rows <= 8
    )


def lane_block(shape, rows):
    return lax.broadcasted_iota(jnp.int32, shape, 1) // rows


def eliminate(systems, rows, group):
    lanes, pieces = systems[0].shape[1], rows // 8
    shape = (8, lanes)
    row_ids = lax.broadcasted_iota(jnp.int32, shape, 0)
    state = [[m[8 * v : 8 * v + 8] for v in range(pieces)] for m in systems]

    def updated(part, column, scale, piece, at):
        pivot = part[piece][at : at + 1] * scale
        fresh = [part[v] - column[v] * pivot for v in range(pieces)]
        fresh[piece] = jnp.where(row_ids == at, pivot, fresh[piece])
        return fresh

    for first in range(0, rows, group):
        columns = [
            [
                [jnp.broadcast_to(p[:, rows + first + t : rows + first + t + 1], shape) for p in m]
                for t in range(group)
            ]
            for m in state
        ]
        for t in range(group):
            piece, at = divmod(first + t, 8)
            for b in range(len(state)):
                column = columns[b][t]
                scale = 1.0 / column[piece][at : at + 1]
                state[b] = updated(state[b], column, scale, piece, at)
                for u in range(t + 1, group):
                    columns[b][u] = updated(columns[b][u], column, scale, piece, at)
    return [jnp.concatenate(m, axis=0) for m in state]


def group_for(count, rows):
    return rows // 2 if count == 1 else rows // 4 if count <= 4 else rows // 8


def merge_segments(tops, bottoms, rows):
    pairs = len(tops) // 2
    solved = eliminate(
        [bottoms[2 * i] + tops[2 * i + 1] for i in range(pairs)], rows, group_for(pairs, rows)
    )
    lanes = solved[0].shape[1]
    block = lane_block(solved[0].shape, rows)
    zero = jnp.zeros((rows, lanes), jnp.float32)
    new_tops, new_bottoms = [], []
    for x, west, east in zip(solved, tops[::2], bottoms[1::2]):
        x_top = jnp.where(block == 0, 0.0, jnp.where(block == 1, pltpu.roll(x, rows, 1), x))
        x_bottom = jnp.where(block == 2, 0.0, jnp.where(block == 1, pltpu.roll(x, lanes - rows, 1), x))
        right = jnp.concatenate([x_bottom, zero, x_top, zero], axis=0)
        change = product(jnp.concatenate([west, east], axis=0), right)
        new_tops.append(jnp.where(block == 2, 0.0, west) - change[:rows])
        new_bottoms.append(jnp.where(block == 0, 0.0, east) - change[rows:])
    return solved, new_tops, new_bottoms


def merge_tree(tops, bottoms, rows, keep):
    while len(tops) > 1:
        solved, tops, bottoms = merge_segments(tops, bottoms, rows)
        keep(solved)
    return tops[0], bottoms[0]


def sublanes(value, by):
    rows = value.shape[0]
    if by % rows % 8:
        return pltpu.roll(value, by % rows, 0)
    by = by % rows
    return jnp.concatenate([value[rows - by :], value[: rows - by]], axis=0)


def solve_lines(middles, links, rights, rows):
    span = 1
    state = list(zip(middles, links, rights))
    while span < rows:
        state = [line_step(*s, span) for s in state]
        span *= 2
    return [right / middle for middle, _, right in state]


def line_step(middle, link, right, span):
    inverse_middle = 1.0 / middle
    down = sublanes(link, -span)
    north = link * sublanes(inverse_middle, span)
    south = down * sublanes(inverse_middle, -span)
    return (
        middle - north * link - south * down,
        north * sublanes(link, span),
        right + north * sublanes(right, span) + south * sublanes(right, -span),
    )


def first_merge(fields_ref, width, rows, maps):
    lanes = fields_ref.shape[1]
    shape = (rows, lanes)
    block = lane_block(shape, rows)
    lane = lax.broadcasted_iota(jnp.int32, shape, 1)
    row = lax.broadcasted_iota(jnp.int32, shape, 0)
    diag0, diag1, diag2 = lane == row, lane == row + rows, lane == row + 2 * rows
    upper = jnp.logical_and(lane == row + rows + 1, block == 1)
    lower = jnp.logical_and(lane == row + rows - 1, block == 1)
    load_lane = jnp.logical_and(lane >= 3 * rows, lane < 3 * rows + maps)
    spare = 3 * rows + maps
    east, diagonal, south, north, load = [], [], [], [], []
    for j in range(width):
        f = fields_ref[j * rows : (j + 1) * rows]
        h = jnp.broadcast_to(f[:, spare + 1 : spare + 2], shape)
        v = jnp.broadcast_to(f[:, spare + 2 : spare + 3], shape)
        va = jnp.where(row == 0, 0.0, pltpu.roll(v, 1, 0))
        east.append(h)
        south.append(v)
        north.append(va)
        diagonal.append(jnp.broadcast_to(f[:, spare : spare + 1], shape) + va + h)
        load.append(jnp.where(load_lane, f, 0.0))
    odd = range(1, width, 2)
    solved = solve_lines(
        [diagonal[j] + east[j - 1] for j in odd],
        [north[j] for j in odd],
        [load[j] - jnp.where(diag0, east[j - 1], 0.0) - jnp.where(diag2, east[j], 0.0) for j in odd],
        rows,
    )
    tops, bottoms = [], []
    for j, x in zip(odd, solved):
        x_top = jnp.where(block == 1, pltpu.roll(x, rows, 1), x)
        x_top = jnp.where(block == 0, 0.0, x_top)
        x_bottom = jnp.where(block == 1, pltpu.roll(x, lanes - rows, 1), x)
        x_bottom = jnp.where(block == 2, 0.0, x_bottom)
        tops.append(
            jnp.where(diag1, diagonal[j - 1], 0.0)
            - jnp.where(upper, south[j - 1], 0.0)
            - jnp.where(lower, north[j - 1], 0.0)
            + load[j - 1]
            + east[j - 1] * x_top
        )
        bottoms.append(jnp.where(diag1, east[j], 0.0) + east[j] * x_bottom)
    return solved, tops, bottoms


def looked_up(x, west, east, rows):
    zero = jnp.zeros_like(west)
    right = jnp.concatenate([west, zero, east, zero], axis=0)
    return jnp.where(lane_block(x.shape, rows) == 3, x, 0.0) - product(x, right)


def node_maps(solved, count, rows, lanes):
    lane = lax.broadcasted_iota(jnp.int32, (rows, lanes), 1)
    row = lax.broadcasted_iota(jnp.int32, (rows, lanes), 0)
    maps = {0: jnp.where(lane == row, -1.0, 0.0), count: jnp.where(lane == row + 2 * rows, -1.0, 0.0)}
    step, level, levels = count // 2, 0, []
    position = 0
    while step >= 1:
        levels.append(position)
        position += count // 2 >> level
        level += 1
        step //= 2
    step = count // 2
    for base in reversed(levels):
        for i, node in enumerate(range(step, count, 2 * step)):
            x = solved(base + i)
            if step == count // 2:
                maps[node] = jnp.where(lane_block(x.shape, rows) == 1, 0.0, x)
            else:
                maps[node] = looked_up(x, maps[node - step], maps[node + step], rows)
        step //= 2
    return maps


def compose(maps_in, x, east, rows):
    block = lane_block(maps_in.shape, rows)
    x = jnp.where(lane_block(x.shape, rows) == 1, 0.0, x)
    zero = jnp.zeros_like(x)
    right = jnp.concatenate([jnp.where(east, x, 0.0), zero, jnp.where(east, 0.0, x), zero], axis=0)
    return jnp.where(block == jnp.where(east, 0, 2), 0.0, maps_in) - product(maps_in, right)


def flipped(me, mask):
    bit = 1
    peer = me
    while bit <= mask:
        if mask // bit % 2:
            peer = peer + bit * (1 - 2 * (me // bit % 2))
        bit *= 2
    return peer


def exchange(axis, source, target, send, recv, mask):
    me = lax.axis_index(axis)
    peer = flipped(me, mask)
    copy = pltpu.make_async_remote_copy(
        src_ref=source(peer),
        dst_ref=target(me),
        send_sem=send.at[mask - 1],
        recv_sem=recv.at[mask - 1],
        device_id={axis: peer},
        device_id_type=MESH,
    )
    copy.start()
    return copy


def build_messages(h_ref, v_ref, c_ref, t_ref, gx_ref, gy_ref, stack_ref, rows, maps, width):
    local_rows, cols = h_ref.shape
    lanes = stack_ref.shape[1]
    lane = lax.broadcasted_iota(jnp.int32, (maps, lanes), 1)
    wide = lambda a: jnp.concatenate([a, jnp.zeros((a.shape[0], lanes - cols), jnp.float32)], axis=1)
    h, v, c = wide(h_ref[...]), wide(v_ref[...]), wide(c_ref[...])
    flux_above = jnp.zeros((maps, lanes), jnp.float32)
    edge = jnp.zeros((maps, lanes), jnp.float32)
    stride = maps + 8
    blank = jnp.zeros((5, lanes), jnp.float32)
    for r in range(local_rows):
        rows_r = pl.ds(r, maps, stride=local_rows)
        along = h[r : r + 1] * wide(gx_ref[rows_r, :])
        flux = v[r : r + 1] * wide(gy_ref[rows_r, :])
        west = jnp.where(lane == 0, 0.0, pltpu.roll(along, 1, 1))
        load = c[r : r + 1] * wide(t_ref[rows_r, :]) + west - along + flux_above - flux
        small = jnp.concatenate([v[r : r + 1] + c[r : r + 1], h[r : r + 1], v[r : r + 1], blank], axis=0)
        stack_ref[r * stride : r * stride + maps] = load
        stack_ref[r * stride + maps : (r + 1) * stride] = small
        place = cols - width + r
        moved = pltpu.roll(along, (place - cols + 1) % lanes, 1)
        edge = jnp.where(lane == place, moved, edge)
        flux_above = flux
    base = 3 * rows
    if local_rows * stride < base:
        stack_ref[local_rows * stride : base] = jnp.zeros((base - local_rows * stride, lanes), jnp.float32)
    stack_ref[base : base + maps] = flux_above
    stack_ref[base + maps : base + 2 * maps] = edge
    if base + 2 * maps < lanes:
        stack_ref[base + 2 * maps :] = jnp.zeros((lanes - base - 2 * maps, lanes), jnp.float32)
    return stack_ref[...].T


def spread_fields(got_ref, fields_ref, edge_ref, rows, maps, width):
    strips, _, lanes = got_ref.shape
    local_rows = rows // strips
    stride, base = maps + 8, 3 * rows
    shape = (width, lanes)
    lane = lax.broadcasted_iota(jnp.int32, shape, 1)
    load_lane = jnp.logical_and(lane >= base, lane < base + maps)
    for s in range(strips):
        part = got_ref[s]
        for r in range(local_rows):
            moved = pltpu.roll(part, (base - r * stride) % lanes, 1)
            if r == 0 and s > 0:
                moved = moved + jnp.where(load_lane, got_ref[s - 1], 0.0)
            for j in range(0, width, 8):
                fields_ref[pl.ds(j * rows + s * local_rows + r, 8, stride=rows), :] = moved[j : j + 8]
        edge_ref[s * local_rows : (s + 1) * local_rows] = pltpu.roll(part, lanes - maps, 1)[:local_rows]


def solve_kernel(
    h_in, v_in, c_in, t_in, gx_in, gy_in, out_ref,
    h_ref, v_ref, c_ref, t_ref, gx_ref, gy_ref, stack_ref, parts_ref, got_ref, fields_ref, edge_ref,
    local_ref, nodes_ref, near_ref, maps_ref, got_maps_ref, pans_ref, path_ref,
    load_sem, send_in, recv_in, send_near, recv_near, send_maps, recv_maps, send_pan, recv_pan,
    *, rows, maps,
):
    strips, me = lax.axis_size("strip"), lax.axis_index("strip")
    panels, panel = lax.axis_size("panel"), lax.axis_index("panel")
    group, width, lanes = parts_ref.shape
    local_rows = rows // strips
    cols = group * width
    barrier = pltpu.get_barrier_semaphore()
    far_first = list(range(strips - 1, 0, -1))
    for mask in far_first:
        pl.semaphore_signal(barrier, inc=1, device_id={"strip": flipped(me, mask)}, device_id_type=MESH)
    for mask in range(1, panels):
        pl.semaphore_signal(barrier, inc=1, device_id={"panel": flipped(panel, mask)}, device_id_type=MESH)
    pairs = zip((h_in, v_in, c_in, t_in, gx_in, gy_in), (h_ref, v_ref, c_ref, t_ref, gx_ref, gy_ref))
    loads = [pltpu.make_async_copy(a, b, load_sem.at[i]) for i, (a, b) in enumerate(pairs)]
    for copy in loads:
        copy.start()
    for copy in loads:
        copy.wait()
    turned = build_messages(h_ref, v_ref, c_ref, t_ref, gx_ref, gy_ref, stack_ref, rows, maps, width)
    for g in range(group):
        parts_ref[g] = turned[g * width : (g + 1) * width]
    pl.semaphore_wait(barrier, strips - 1 + panels - 1)

    first = [
        exchange("strip", lambda p: parts_ref.at[p % group], lambda m: got_ref.at[m], send_in, recv_in, mask)
        for mask in far_first
    ]
    mine = me % group
    got_ref[me] = parts_ref[mine]
    for copy in reversed(first):
        copy.wait_recv()
    spread_fields(got_ref, fields_ref, edge_ref, rows, maps, width)
    solved, tops, bottoms = first_merge(fields_ref, width, rows, maps)
    kept = [0]

    def keep(xs):
        for x in xs:
            local_ref[kept[0]] = x
            kept[0] += 1

    keep(solved)
    lane = lax.broadcasted_iota(jnp.int32, (rows, lanes), 1)
    load_lane = jnp.logical_and(lane >= 3 * rows, lane < 3 * rows + maps)
    last_edge = jnp.logical_and(load_lane, mine == group - 1)
    bottoms[-1] = bottoms[-1] + jnp.where(last_edge, edge_ref[...], 0.0)
    top, bottom = merge_tree(tops, bottoms, rows, keep)
    near_ref[mine, :rows] = top
    near_ref[mine, rows:] = bottom
    near = [
        exchange("strip", lambda p: near_ref.at[mine], lambda m: near_ref.at[m % group], send_near, recv_near, mask)
        for mask in range(group - 1, 0, -1)
    ]

    columns = node_maps(lambda i: local_ref[i], width, rows, lanes)
    start = pl.multiple_of((me - mine) * local_rows, group * local_rows)
    for j in range(width):
        nodes_ref[j] = columns[j]
    for j in range(width):
        picked = nodes_ref[j, pl.ds(start, group * local_rows)]
        maps_ref[pl.ds(j, group * local_rows, stride=width), :] = picked
    size = width * local_rows
    spans = lambda p: maps_ref.at[pl.ds(pl.multiple_of(p % group * size, size), size)]
    moved = [
        exchange("strip", spans, lambda m: got_maps_ref.at[m % group], send_maps, recv_maps, mask)
        for mask in range(group - 1, 0, -1)
    ]
    got_maps_ref[mine] = maps_ref[pl.ds(pl.multiple_of(mine * size, size), size)]

    for copy in near:
        copy.wait_recv()
    tops = [near_ref[g, :rows] for g in range(group)]
    bottoms = [near_ref[g, rows:] for g in range(group)]
    inner = []
    top, bottom = merge_tree(tops, bottoms, rows, inner.extend)
    pans_ref[panel, :rows] = top
    pans_ref[panel, rows:] = bottom
    across = [
        exchange("panel", lambda p: pans_ref.at[panel], lambda m: pans_ref.at[m], send_pan, recv_pan, mask)
        for mask in range(1, panels)
    ]
    ends = node_maps(lambda i: inner[i], group, rows, lanes)
    for copy in moved:
        copy.wait_recv()
    for g in range(group):
        part = looked_up(got_maps_ref[g], ends[g], ends[g + 1], rows)
        for r in range(local_rows):
            path_ref[r * cols + g * width : r * cols + (g + 1) * width] = part[r * width : (r + 1) * width]
    for copy in across:
        copy.wait_recv()
    tops = [pans_ref[p, :rows] for p in range(panels)]
    bottoms = [pans_ref[p, rows:] for p in range(panels)]
    path, spot = path_ref[...], panel
    while len(tops) > 1:
        solved, tops, bottoms = merge_segments(tops, bottoms, rows)
        chosen = solved[0]
        for i in range(1, len(solved)):
            chosen = jnp.where(spot // 2 == i, solved[i], chosen)
        path = compose(path, chosen, spot % 2 == 1, rows)
        spot = spot // 2
    top, bottom = tops[0], bottoms[0]
    block = lane_block((rows, lanes), rows)
    wrap = pltpu.roll(top, lanes - rows, 1) + pltpu.roll(bottom, rows, 1)
    closing = top + bottom + jnp.where(block == 1, wrap, 0.0)
    final = eliminate([closing], rows, rows // 2)[0]
    turned = path.T
    weight = turned[:rows] + turned[2 * rows : 3 * rows]
    values = final.T[3 * rows : 3 * rows + maps]
    result = turned[3 * rows : 3 * rows + maps] - product(values, weight)
    for r in range(local_rows):
        out_ref[pl.ds(r, maps, stride=local_rows), :] = result[:, r * cols : (r + 1) * cols]
    for copy in first + near + moved + across:
        copy.wait_send()


def longitude_shards(h_cond, v_cond, confidence, teacher, grad_x, grad_y):
    local_rows, cols = h_cond.shape
    maps = teacher.shape[0]
    strips, panels = lax.axis_size("strip"), lax.axis_size("panel")
    rows, lanes = local_rows * strips, 4 * local_rows * strips
    group = strips // SHARED
    width = cols // group
    f32 = jnp.float32
    dma = pltpu.SemaphoreType.DMA
    flat = (maps * local_rows, cols)
    size = width * local_rows
    values = pl.pallas_call(
        functools.partial(solve_kernel, rows=rows, maps=maps),
        out_shape=pltpu.VMEM(flat, f32),
        in_specs=[pl.BlockSpec(memory_space=pl.ANY)] * 6,
        out_specs=pl.BlockSpec(memory_space=pltpu.VMEM),
        scratch_shapes=[
            pltpu.VMEM((local_rows, cols), f32),
            pltpu.VMEM((local_rows, cols), f32),
            pltpu.VMEM((local_rows, cols), f32),
            pltpu.VMEM(flat, f32),
            pltpu.VMEM(flat, f32),
            pltpu.VMEM(flat, f32),
            pltpu.VMEM((lanes, lanes), f32),
            pltpu.VMEM((group, width, lanes), f32),
            pltpu.VMEM((strips, width, lanes), f32),
            pltpu.VMEM((width * rows, lanes), f32),
            pltpu.VMEM((rows, lanes), f32),
            pltpu.VMEM((width - 1, rows, lanes), f32),
            pltpu.VMEM((width, rows, lanes), f32),
            pltpu.VMEM((group, 2 * rows, lanes), f32),
            pltpu.VMEM((group * size, lanes), f32),
            pltpu.VMEM((group, size, lanes), f32),
            pltpu.VMEM((panels, 2 * rows, lanes), f32),
            pltpu.VMEM((local_rows * cols, lanes), f32),
            dma((6,)),
            dma((strips - 1,)),
            dma((strips - 1,)),
            dma((group - 1,)),
            dma((group - 1,)),
            dma((group - 1,)),
            dma((group - 1,)),
            dma((panels - 1,)),
            dma((panels - 1,)),
        ],
        compiler_params=pltpu.CompilerParams(collective_id=0, has_side_effects=True),
    )(h_cond, v_cond, confidence, *(a.reshape(flat) for a in (teacher, grad_x, grad_y)))
    return values.reshape(maps, local_rows, cols)


def shards(h_cond, v_cond, confidence, teacher, grad_x, grad_y):
    strips, panels = lax.axis_size("strip"), lax.axis_size("panel")
    fits = tall_enough(h_cond.shape, teacher.shape[0], strips, panels)
    body = longitude_shards if fits else latitude_shards
    return body(h_cond, v_cond, confidence, teacher, grad_x, grad_y)


def solution(mesh):
    in_specs = (
        P("strip", "panel"),
        P("strip", "panel"),
        P("strip", "panel"),
        P(None, "strip", "panel"),
        P(None, "strip", "panel"),
        P(None, "strip", "panel"),
    )
    out_specs = P(None, "strip", "panel")
    return jax.shard_map(shards, mesh=mesh, in_specs=in_specs, out_specs=out_specs, check_vma=False)
```

```python
import functools

import jax
import jax.numpy as jnp
from jax import lax
from jax.experimental import pallas as pl
from jax.experimental.pallas import tpu as pltpu
from jax.sharding import PartitionSpec as P

HIGH = lax.Precision.HIGHEST


def shifted(value, axis, by):
    count = lax.axis_size(axis)
    pairs = [(i, i + by) for i in range(count) if 0 <= i + by < count]
    return lax.ppermute(value, axis, pairs)


def carried_in(value, axis, join, neutral, backward):
    count, mine = (lax.axis_size(axis), lax.axis_index(axis))
    pieces = jax.tree.map(lambda part: lax.all_gather(part, axis), value)
    if backward:
        pieces = jax.tree.map(lambda part: part[::-1], pieces)
        mine = count - 1 - mine
    total = jax.tree.map(
        lambda part, zero: jnp.full_like(part, 0) + jnp.asarray(zero, part.dtype), value, neutral
    )

    def turn(position, total):
        longer = join(total, jax.tree.map(lambda part: part[position], pieces))
        return jax.tree.map(lambda new, old: jnp.where(position < mine, new, old), longer, total)

    return lax.fori_loop(0, count - 1, turn, total)


def product(left, right):
    return jnp.dot(left, right, precision=HIGH, preferred_element_type=jnp.float32)


def apply_to(matrix, vectors):
    return product(vectors, matrix.T)


def row_matrix(diag_row, link_row):
    extent = diag_row.shape[0]
    row_ids = lax.broadcasted_iota(jnp.int32, (extent, extent), 0)
    col_ids = lax.broadcasted_iota(jnp.int32, (extent, extent), 1)
    east = col_ids == (row_ids + 1) % extent
    west = row_ids == (col_ids + 1) % extent
    link = jnp.where(east, link_row[:, None], 0.0) + jnp.where(west, link_row[None, :], 0.0)
    return jnp.where(row_ids == col_ids, diag_row[:, None], 0.0) - link


def inverse(matrix):
    factor = jnp.linalg.cholesky(matrix)
    return jax.scipy.linalg.cho_solve((factor, True), jnp.eye(matrix.shape[0], dtype=jnp.float32))


def load_update(factor, upper, lower):
    vector = jax.scipy.linalg.cho_solve((factor, True), (upper[4] + lower[3]).T)
    return (upper[3] - product(upper[1], vector).T, lower[4] - product(lower[1].T, vector).T)


def merge_whole(upper, lower):
    extent = upper[2].shape[0]
    factor = jnp.linalg.cholesky(upper[2] + lower[0])
    solved = jax.scipy.linalg.cho_solve(
        (factor, True), jnp.concatenate([upper[1].T, lower[1]], axis=1)
    )
    first_cols = solved[:, :extent]
    second_cols = solved[:, extent:]
    first_load, second_load = load_update(factor, upper, lower)
    return (
        upper[0] - product(upper[1], first_cols),
        -product(upper[1], second_cols),
        lower[2] - product(lower[1].T, second_cols),
        first_load,
        second_load,
    )


def merge_flagged(upper, lower):
    merged = merge_whole(upper[:5], lower[:5])
    upper_empty = upper[5] > 0.5
    lower_empty = lower[5] > 0.5
    picked = tuple(
        (
            jnp.where(upper_empty, lower_part, jnp.where(lower_empty, upper_part, merged_part))
            for upper_part, lower_part, merged_part in zip(upper[:5], lower[:5], merged)
        )
    )
    return picked + (upper[5] * lower[5],)


def chain_maps(earlier_map, later_map):
    return (
        product(later_map[0], earlier_map[0]),
        later_map[1] + apply_to(later_map[0], earlier_map[1]),
    )


def substitute(value_below, inputs):
    gain, offset = inputs
    value = offset + apply_to(gain, value_below)
    return (value, value)


def latitude_shards(h_cond, v_cond, confidence, teacher, grad_x, grad_y):
    slice_cols = h_cond.shape[1]
    local_rows = h_cond.shape[0]
    hypotheses = teacher.shape[0]
    edge_rows = jnp.concatenate([v_cond[-1][None], v_cond[-1][None] * grad_y[:, -1]], axis=0)
    above = shifted(edge_rows, "strip", 1)
    packed = jnp.concatenate(
        [
            h_cond,
            v_cond,
            confidence,
            above,
            teacher.reshape(hypotheses * local_rows, slice_cols),
            grad_x.reshape(hypotheses * local_rows, slice_cols),
            grad_y.reshape(hypotheses * local_rows, slice_cols),
        ],
        axis=0,
    )
    whole = lax.all_gather(packed, "panel", axis=1, tiled=True)
    extent = whole.shape[1]
    horizontal = whole[:local_rows]
    vertical = whole[local_rows : 2 * local_rows]
    weights = whole[2 * local_rows : 3 * local_rows]
    vertical_edge = whole[3 * local_rows]
    flux_edge = whole[3 * local_rows + 1 : 3 * local_rows + 1 + hypotheses]
    base = 3 * local_rows + 1 + hypotheses
    stride = hypotheses * local_rows
    targets = whole[base : base + stride].reshape(hypotheses, local_rows, extent)
    slope_x = whole[base + stride : base + 2 * stride].reshape(hypotheses, local_rows, extent)
    slope_y = whole[base + 2 * stride : base + 3 * stride].reshape(hypotheses, local_rows, extent)
    vertical_above = jnp.concatenate([vertical_edge[None], vertical[:-1]], axis=0)
    flux = vertical[None] * slope_y
    flux_above = jnp.concatenate([flux_edge[:, None], flux[:, :-1]], axis=1)
    along = horizontal[None] * slope_x
    loads = weights[None] * targets + jnp.roll(along, 1, axis=2) - along + flux_above - flux
    loads = jnp.transpose(loads, (1, 0, 2))
    diagonal = jnp.roll(horizontal, 1, axis=1) + horizontal + vertical_above + vertical + weights
    blocks = jax.vmap(row_matrix)(diagonal, horizontal)
    zeros_mat = jnp.zeros((extent, extent), jnp.float32)
    zeros_vec = jnp.zeros((hypotheses, extent), jnp.float32)
    identity = jnp.eye(extent, dtype=jnp.float32)
    start = (zeros_mat, -jnp.diag(vertical_above[0]), blocks[0], zeros_vec, loads[0])

    def fold_step(segment, inputs):
        matrix_row, coupling, load_row = inputs
        piece = (zeros_mat, -jnp.diag(coupling), matrix_row, zeros_vec, load_row)
        merged = merge_whole(segment, piece)
        return (merged, None)

    segment, _ = lax.scan(fold_step, start, (blocks[1:], vertical_above[1:], loads[1:]))
    filled = segment + (jnp.zeros((), jnp.float32),)
    blank = (zeros_mat, zeros_mat, identity, zeros_vec, zeros_vec, jnp.ones((), jnp.float32))
    prefix = carried_in(filled, "strip", merge_flagged, blank, False)
    prefix_matrix, prefix_load = (prefix[2], prefix[4])

    def eliminate(state, inputs):
        inverse_prev, load_prev, pivot_prev = state
        matrix_row, coupling, load_row, coupling_below = inputs
        pivot = matrix_row - coupling[:, None] * inverse_prev * coupling[None, :]
        carried = load_row + coupling[None, :] * apply_to(inverse_prev, load_prev)
        inverse_now = inverse(pivot)
        return (
            (inverse_now, carried, pivot),
            (inverse_now * coupling_below[None, :], apply_to(inverse_now, carried)),
        )

    final_state, (gains, offsets) = lax.scan(
        eliminate,
        (inverse(prefix_matrix), prefix_load, identity),
        (blocks, vertical_above, loads, vertical),
    )

    def compose(mapping, inputs):
        gain, offset = inputs
        return ((product(gain, mapping[0]), offset + apply_to(gain, mapping[1])), None)

    (reach, moved), _ = lax.scan(compose, (identity, zeros_vec), (gains, offsets), reverse=True)
    beyond = carried_in((reach, moved), "strip", chain_maps, (identity, zeros_vec), True)
    _, solution = lax.scan(substitute, beyond[1], (gains, offsets), reverse=True)
    solution = jnp.transpose(solution, (1, 0, 2))
    return lax.dynamic_slice_in_dim(solution, lax.axis_index("panel") * slice_cols, slice_cols, 2)


SHARED = 2
MESH = pl.DeviceIdType.MESH


def power_of_two(n):
    return n >= 2 and n & (n - 1) == 0


def tall_enough(shape, maps, strips, panels):
    local_rows, cols = shape
    rows, group = local_rows * strips, strips // SHARED
    if not (power_of_two(strips) and panels in (2, 4) and group >= 2 and cols % group == 0):
        return False
    width = cols // group
    lanes = 4 * rows
    return (
        lanes == 128
        and cols <= lanes
        and local_rows >= 3
        and power_of_two(width)
        and width % 8 == 0
        and maps % 8 == 0
        and 2 * maps <= rows
        and local_rows * (maps + 8) <= 3 * rows
        and local_rows <= 8
    )


def lane_block(shape, rows):
    return lax.broadcasted_iota(jnp.int32, shape, 1) // rows


def eliminate(systems, spots, rows, group):
    lanes, pieces = systems[0].shape[1], rows // 8
    shape = (8, lanes)
    row_ids = lax.broadcasted_iota(jnp.int32, shape, 0)
    state = [[m[8 * v : 8 * v + 8] for v in range(pieces)] for m in systems]
    for first in range(0, rows, group):
        columns = [
            [
                [jnp.broadcast_to(p[:, at : at + 1], shape) for p in m]
                for at in range(spot * rows + first, spot * rows + first + group)
            ]
            for m, spot in zip(state, spots)
        ]
        for t in range(group):
            piece, at = divmod(first + t, 8)
            for b in range(len(state)):
                column = columns[b][t]
                scale = 1.0 / column[piece][at : at + 1]
                factors = list(column)
                factors[piece] = jnp.where(row_ids == at, column[piece] - 1.0, column[piece])

                def updated(part):
                    pivot = part[piece][at : at + 1] * scale
                    return [part[v] - factors[v] * pivot for v in range(pieces)]

                state[b] = updated(state[b])
                for u in range(t + 1, group):
                    columns[b][u] = updated(columns[b][u])
    return [jnp.concatenate(m, axis=0) for m in state]


def group_for(count, rows):
    return rows // 2 if count == 1 else rows // 4 if count == 2 else rows // 8


def halves(frame):
    west, middle, east = frame
    return (west, east, middle), (middle, west, east)


def frames_for(count):
    levels, frames = [], [(0, 2, 1)]
    while len(frames) < count:
        levels.append(frames)
        frames = [half for frame in frames for half in halves(frame)]
    return levels[::-1]


def placed(segment, west, east, rows):
    lanes = segment.shape[1]
    block = lane_block(segment.shape, rows)
    at_west = segment if west == 0 else pltpu.roll(segment, west * rows, 1)
    at_east = segment if east == 1 else pltpu.roll(segment, (east - 1) * rows % lanes, 1)
    rest = jnp.where(block == 3, segment, 0.0)
    return jnp.where(block == west, at_west, jnp.where(block == east, at_east, rest))


def span_of(left, spot, rows):
    return left[:, spot * rows : (spot + 1) * rows]


def merge_segments(tops, bottoms, frames, rows):
    spots = [frame[1] for frame in frames]
    pairs = len(frames)
    solved = eliminate(
        [bottoms[2 * i] + tops[2 * i + 1] for i in range(pairs)], spots, rows, group_for(pairs, rows)
    )
    new_tops, new_bottoms = [], []
    for x, spot, west, east in zip(solved, spots, tops[::2], bottoms[1::2]):
        left = jnp.concatenate([west, east], axis=0)
        merged = left - product(span_of(left, spot, rows), x)
        merged = jnp.where(lane_block(merged.shape, rows) == spot, 0.0, merged)
        new_tops.append(merged[:rows])
        new_bottoms.append(merged[rows:])
    return solved, new_tops, new_bottoms


def merge_tree(tops, bottoms, levels, rows, keep):
    for frames in levels:
        solved, tops, bottoms = merge_segments(tops, bottoms, frames, rows)
        keep(solved)
    return tops, bottoms


def sublanes(value, by):
    rows = value.shape[0]
    if by % rows % 8:
        return pltpu.roll(value, by % rows, 0)
    by = by % rows
    return jnp.concatenate([value[rows - by :], value[: rows - by]], axis=0)


def solve_lines(middles, links, rights, rows):
    span = 1
    state = list(zip(middles, links, rights))
    while span < rows:
        state = [line_step(*s, span) for s in state]
        span *= 2
    return [right / middle for middle, _, right in state]


def line_step(middle, link, right, span):
    inverse_middle = 1.0 / middle
    down = sublanes(link, -span)
    north = link * sublanes(inverse_middle, span)
    south = down * sublanes(inverse_middle, -span)
    return (
        middle - north * link - south * down,
        north * sublanes(link, span),
        right + north * sublanes(right, span) + south * sublanes(right, -span),
    )


def first_merge(fields_ref, frames, rows, maps):
    width = 2 * len(frames)
    lanes = fields_ref.shape[1]
    shape = (rows, lanes)
    block = lane_block(shape, rows)
    lane = lax.broadcasted_iota(jnp.int32, shape, 1)
    row = lax.broadcasted_iota(jnp.int32, shape, 0)
    diagonals = [lane == row + spot * rows for spot in range(3)]
    uppers = [jnp.logical_and(lane == row + spot * rows + 1, block == spot) for spot in range(3)]
    lowers = [jnp.logical_and(lane == row + spot * rows - 1, block == spot) for spot in range(3)]
    load_lane = jnp.logical_and(lane >= 3 * rows, lane < 3 * rows + maps)
    spare = 3 * rows + maps
    east, diagonal, south, north, load = [], [], [], [], []
    for j in range(width):
        f = fields_ref[j * rows : (j + 1) * rows]
        h = jnp.broadcast_to(f[:, spare + 1 : spare + 2], shape)
        v = jnp.broadcast_to(f[:, spare + 2 : spare + 3], shape)
        va = jnp.where(row == 0, 0.0, pltpu.roll(v, 1, 0))
        east.append(h)
        south.append(v)
        north.append(va)
        diagonal.append(jnp.broadcast_to(f[:, spare : spare + 1], shape) + va + h)
        load.append(jnp.where(load_lane, f, 0.0))
    odd = range(1, width, 2)
    solved = solve_lines(
        [diagonal[j] + east[j - 1] for j in odd],
        [north[j] for j in odd],
        [
            load[j]
            - jnp.where(diagonals[frame[0]], east[j - 1], 0.0)
            - jnp.where(diagonals[frame[2]], east[j], 0.0)
            for j, frame in zip(odd, frames)
        ],
        rows,
    )
    tops, bottoms = [], []
    for j, x, (west, _, far) in zip(odd, solved, frames):
        tops.append(
            jnp.where(diagonals[west], diagonal[j - 1], 0.0)
            - jnp.where(uppers[west], south[j - 1], 0.0)
            - jnp.where(lowers[west], north[j - 1], 0.0)
            + load[j - 1]
            + east[j - 1] * x
        )
        bottoms.append(jnp.where(diagonals[far], east[j], 0.0) + east[j] * x)
    return solved, tops, bottoms


def looked_up(x, frame, west, east, rows):
    parts = {frame[0]: west, frame[1]: jnp.zeros_like(west), frame[2]: east}
    right = jnp.concatenate([parts[spot] for spot in range(3)], axis=0)
    return jnp.where(lane_block(x.shape, rows) == 3, x, 0.0) - product(x[:, : 3 * rows], right)


def node_maps(solved, levels, rows, lanes):
    count = 2 * len(levels[0])
    lane = lax.broadcasted_iota(jnp.int32, (rows, lanes), 1)
    row = lax.broadcasted_iota(jnp.int32, (rows, lanes), 0)
    maps = {0: jnp.where(lane == row, -1.0, 0.0), count: jnp.where(lane == row + rows, -1.0, 0.0)}
    position, step = sum(len(frames) for frames in levels), count // 2
    for frames in levels[::-1]:
        position -= len(frames)
        for i, frame in enumerate(frames):
            node = step * (2 * i + 1)
            maps[node] = looked_up(solved(position + i), frame, maps[node - step], maps[node + step], rows)
        step //= 2
    return maps


def compose(maps_in, x, spot, rows):
    x = jnp.where(lane_block(x.shape, rows) == spot, 0.0, x)
    zero = jnp.zeros_like(x)
    right = jnp.concatenate([zero] * spot + [x], axis=0)
    change = product(maps_in[:, : (spot + 1) * rows], right)
    return jnp.where(lane_block(maps_in.shape, rows) == spot, 0.0, maps_in) - change


def flipped(me, mask):
    bit = 1
    peer = me
    while bit <= mask:
        if mask // bit % 2:
            peer = peer + bit * (1 - 2 * (me // bit % 2))
        bit *= 2
    return peer


def exchange(axis, source, target, send, recv, mask):
    me = lax.axis_index(axis)
    peer = flipped(me, mask)
    copy = pltpu.make_async_remote_copy(
        src_ref=source(peer),
        dst_ref=target(me),
        send_sem=send.at[mask - 1],
        recv_sem=recv.at[mask - 1],
        device_id={axis: peer},
        device_id_type=MESH,
    )
    copy.start()
    return copy


def build_messages(h_ref, v_ref, c_ref, t_ref, gx_ref, gy_ref, stack_ref, rows, maps, width):
    local_rows, cols = h_ref.shape
    lanes = stack_ref.shape[1]
    lane = lax.broadcasted_iota(jnp.int32, (maps, lanes), 1)
    wide = lambda a: jnp.concatenate([a, jnp.zeros((a.shape[0], lanes - cols), jnp.float32)], axis=1)
    h, v, c = wide(h_ref[...]), wide(v_ref[...]), wide(c_ref[...])
    flux_above = jnp.zeros((maps, lanes), jnp.float32)
    edge = jnp.zeros((maps, lanes), jnp.float32)
    stride = maps + 8
    blank = jnp.zeros((5, lanes), jnp.float32)
    for r in range(local_rows):
        rows_r = pl.ds(r, maps, stride=local_rows)
        along = h[r : r + 1] * wide(gx_ref[rows_r, :])
        flux = v[r : r + 1] * wide(gy_ref[rows_r, :])
        west = jnp.where(lane == 0, 0.0, pltpu.roll(along, 1, 1))
        load = c[r : r + 1] * wide(t_ref[rows_r, :]) + west - along + flux_above - flux
        small = jnp.concatenate([v[r : r + 1] + c[r : r + 1], h[r : r + 1], v[r : r + 1], blank], axis=0)
        stack_ref[r * stride : r * stride + maps] = load
        stack_ref[r * stride + maps : (r + 1) * stride] = small
        place = cols - width + r
        moved = pltpu.roll(along, (place - cols + 1) % lanes, 1)
        edge = jnp.where(lane == place, moved, edge)
        flux_above = flux
    base = 3 * rows
    if local_rows * stride < base:
        stack_ref[local_rows * stride : base] = jnp.zeros((base - local_rows * stride, lanes), jnp.float32)
    stack_ref[base : base + maps] = flux_above
    stack_ref[base + maps : base + 2 * maps] = edge
    if base + 2 * maps < lanes:
        stack_ref[base + 2 * maps :] = jnp.zeros((lanes - base - 2 * maps, lanes), jnp.float32)
    return stack_ref[...].T


def spread_fields(got_ref, fields_ref, edge_ref, rows, maps, width):
    strips, _, lanes = got_ref.shape
    local_rows = rows // strips
    stride, base = maps + 8, 3 * rows
    shape = (width, lanes)
    lane = lax.broadcasted_iota(jnp.int32, shape, 1)
    load_lane = jnp.logical_and(lane >= base, lane < base + maps)
    for s in range(strips):
        part = got_ref[s]
        for r in range(local_rows):
            moved = pltpu.roll(part, (base - r * stride) % lanes, 1)
            if r == 0 and s > 0:
                moved = moved + jnp.where(load_lane, got_ref[s - 1], 0.0)
            for j in range(0, width, 8):
                fields_ref[pl.ds(j * rows + s * local_rows + r, 8, stride=rows), :] = moved[j : j + 8]
        edge_ref[s * local_rows : (s + 1) * local_rows] = pltpu.roll(part, lanes - maps, 1)[:local_rows]


def solve_kernel(
    h_in, v_in, c_in, t_in, gx_in, gy_in, out_ref,
    h_ref, v_ref, c_ref, t_ref, gx_ref, gy_ref, stack_ref, parts_ref, got_ref, fields_ref, edge_ref,
    local_ref, nodes_ref, near_ref, maps_ref, got_maps_ref, pans_ref, path_ref,
    load_sem, send_in, recv_in, send_near, recv_near, send_maps, recv_maps, send_pan, recv_pan,
    *, rows, maps,
):
    strips, me = lax.axis_size("strip"), lax.axis_index("strip")
    panels, panel = lax.axis_size("panel"), lax.axis_index("panel")
    group, width, lanes = parts_ref.shape
    local_rows = rows // strips
    cols = group * width
    barrier = pltpu.get_barrier_semaphore()
    far_first = list(range(strips - 1, 0, -1))
    for mask in far_first:
        pl.semaphore_signal(barrier, inc=1, device_id={"strip": flipped(me, mask)}, device_id_type=MESH)
    for mask in range(1, panels):
        pl.semaphore_signal(barrier, inc=1, device_id={"panel": flipped(panel, mask)}, device_id_type=MESH)
    pairs = zip((h_in, v_in, c_in, t_in, gx_in, gy_in), (h_ref, v_ref, c_ref, t_ref, gx_ref, gy_ref))
    loads = [pltpu.make_async_copy(a, b, load_sem.at[i]) for i, (a, b) in enumerate(pairs)]
    for copy in loads:
        copy.start()
    for copy in loads:
        copy.wait()
    turned = build_messages(h_ref, v_ref, c_ref, t_ref, gx_ref, gy_ref, stack_ref, rows, maps, width)
    for g in range(group):
        parts_ref[g] = turned[g * width : (g + 1) * width]
    pl.semaphore_wait(barrier, strips - 1 + panels - 1)

    first = [
        exchange("strip", lambda p: parts_ref.at[p % group], lambda m: got_ref.at[m], send_in, recv_in, mask)
        for mask in far_first
    ]
    mine = me % group
    got_ref[me] = parts_ref[mine]
    for copy in reversed(first):
        copy.wait_recv()
    spread_fields(got_ref, fields_ref, edge_ref, rows, maps, width)
    levels = frames_for(width)
    solved, tops, bottoms = first_merge(fields_ref, levels[0], rows, maps)
    kept = [0]

    def keep(xs):
        for x in xs:
            local_ref[kept[0]] = x
            kept[0] += 1

    keep(solved)
    lane = lax.broadcasted_iota(jnp.int32, (rows, lanes), 1)
    load_lane = jnp.logical_and(lane >= 3 * rows, lane < 3 * rows + maps)
    last_edge = jnp.logical_and(load_lane, mine == group - 1)
    bottoms[-1] = bottoms[-1] + jnp.where(last_edge, edge_ref[...], 0.0)
    (top,), (bottom,) = merge_tree(tops, bottoms, levels[1:], rows, keep)
    near_ref[mine, :rows] = top
    near_ref[mine, rows:] = bottom
    near = [
        exchange("strip", lambda p: near_ref.at[mine], lambda m: near_ref.at[m % group], send_near, recv_near, mask)
        for mask in range(group - 1, 0, -1)
    ]

    columns = node_maps(lambda i: local_ref[i], levels, rows, lanes)
    start = pl.multiple_of((me - mine) * local_rows, group * local_rows)
    for j in range(width):
        nodes_ref[j] = columns[j]
    for j in range(width):
        picked = nodes_ref[j, pl.ds(start, group * local_rows)]
        maps_ref[pl.ds(j, group * local_rows, stride=width), :] = picked
    size = width * local_rows
    spans = lambda p: maps_ref.at[pl.ds(pl.multiple_of(p % group * size, size), size)]
    moved = [
        exchange("strip", spans, lambda m: got_maps_ref.at[m % group], send_maps, recv_maps, mask)
        for mask in range(group - 1, 0, -1)
    ]
    got_maps_ref[mine] = maps_ref[pl.ds(pl.multiple_of(mine * size, size), size)]

    for copy in near:
        copy.wait_recv()
    levels = frames_for(group)
    tops, bottoms = [], []
    for g in range(group):
        half = halves(levels[0][g // 2])[g % 2]
        both = placed(near_ref[g], half[0], half[2], rows)
        tops.append(both[:rows])
        bottoms.append(both[rows:])
    inner = []
    (top,), (bottom,) = merge_tree(tops, bottoms, levels, rows, inner.extend)
    pans_ref[panel, :rows] = top
    pans_ref[panel, rows:] = bottom
    across = [
        exchange("panel", lambda p: pans_ref.at[panel], lambda m: pans_ref.at[m], send_pan, recv_pan, mask)
        for mask in range(1, panels)
    ]
    spots = [(0, 1), (1, 2), (2, 1), (1, 0)] if panels > 2 else [(0, 2), (2, 0)]
    ends = node_maps(lambda i: inner[i], levels, rows, lanes)
    for g in range(group + 1):
        choice = placed(ends[g], *spots[0], rows)
        for p in range(1, panels):
            choice = jnp.where(panel == p, placed(ends[g], *spots[p], rows), choice)
        ends[g] = choice
    for copy in moved:
        copy.wait_recv()
    for g in range(group):
        part = looked_up(got_maps_ref[g], (0, 2, 1), ends[g], ends[g + 1], rows)
        for r in range(local_rows):
            path_ref[r * cols + g * width : r * cols + (g + 1) * width] = part[r * width : (r + 1) * width]
    for copy in across:
        copy.wait_recv()
    tops, bottoms = [], []
    for p in range(panels):
        both = placed(pans_ref[p], *spots[p], rows)
        tops.append(both[:rows])
        bottoms.append(both[rows:])
    path = path_ref[...]
    if panels > 2:
        solved, tops, bottoms = merge_segments(tops, bottoms, [(0, 1, 2), (2, 1, 0)], rows)
        path = compose(path, jnp.where(panel < 2, solved[0], solved[1]), 1, rows)
    middle = eliminate([bottoms[0] + tops[1]], [2], rows, group_for(1, rows))[0]
    around = tops[0] + bottoms[1]
    closing = around - product(span_of(around, 2, rows), middle)
    final = eliminate([closing], [0], rows, group_for(1, rows))[0]
    turned = compose(path, middle, 2, rows).T
    weight = turned[:rows]
    values = final.T[3 * rows : 3 * rows + maps]
    result = turned[3 * rows : 3 * rows + maps] - product(values, weight)
    for r in range(local_rows):
        out_ref[pl.ds(r, maps, stride=local_rows), :] = result[:, r * cols : (r + 1) * cols]
    for copy in first + near + moved + across:
        copy.wait_send()


def longitude_shards(h_cond, v_cond, confidence, teacher, grad_x, grad_y):
    local_rows, cols = h_cond.shape
    maps = teacher.shape[0]
    strips, panels = lax.axis_size("strip"), lax.axis_size("panel")
    rows, lanes = local_rows * strips, 4 * local_rows * strips
    group = strips // SHARED
    width = cols // group
    f32 = jnp.float32
    dma = pltpu.SemaphoreType.DMA
    flat = (maps * local_rows, cols)
    size = width * local_rows
    values = pl.pallas_call(
        functools.partial(solve_kernel, rows=rows, maps=maps),
        out_shape=pltpu.VMEM(flat, f32),
        in_specs=[pl.BlockSpec(memory_space=pl.ANY)] * 6,
        out_specs=pl.BlockSpec(memory_space=pltpu.VMEM),
        scratch_shapes=[
            pltpu.VMEM((local_rows, cols), f32),
            pltpu.VMEM((local_rows, cols), f32),
            pltpu.VMEM((local_rows, cols), f32),
            pltpu.VMEM(flat, f32),
            pltpu.VMEM(flat, f32),
            pltpu.VMEM(flat, f32),
            pltpu.VMEM((lanes, lanes), f32),
            pltpu.VMEM((group, width, lanes), f32),
            pltpu.VMEM((strips, width, lanes), f32),
            pltpu.VMEM((width * rows, lanes), f32),
            pltpu.VMEM((rows, lanes), f32),
            pltpu.VMEM((width - 1, rows, lanes), f32),
            pltpu.VMEM((width, rows, lanes), f32),
            pltpu.VMEM((group, 2 * rows, lanes), f32),
            pltpu.VMEM((group * size, lanes), f32),
            pltpu.VMEM((group, size, lanes), f32),
            pltpu.VMEM((panels, 2 * rows, lanes), f32),
            pltpu.VMEM((local_rows * cols, lanes), f32),
            dma((6,)),
            dma((strips - 1,)),
            dma((strips - 1,)),
            dma((group - 1,)),
            dma((group - 1,)),
            dma((group - 1,)),
            dma((group - 1,)),
            dma((panels - 1,)),
            dma((panels - 1,)),
        ],
        compiler_params=pltpu.CompilerParams(collective_id=0, has_side_effects=True),
    )(h_cond, v_cond, confidence, *(a.reshape(flat) for a in (teacher, grad_x, grad_y)))
    return values.reshape(maps, local_rows, cols)


def shards(h_cond, v_cond, confidence, teacher, grad_x, grad_y):
    strips, panels = lax.axis_size("strip"), lax.axis_size("panel")
    fits = tall_enough(h_cond.shape, teacher.shape[0], strips, panels)
    body = longitude_shards if fits else latitude_shards
    return body(h_cond, v_cond, confidence, teacher, grad_x, grad_y)


def solution(mesh):
    in_specs = (
        P("strip", "panel"),
        P("strip", "panel"),
        P("strip", "panel"),
        P(None, "strip", "panel"),
        P(None, "strip", "panel"),
        P(None, "strip", "panel"),
    )
    out_specs = P(None, "strip", "panel")
    return jax.shard_map(shards, mesh=mesh, in_specs=in_specs, out_specs=out_specs, check_vma=False)
```

```python
import functools

import jax
import jax.numpy as jnp
from jax import lax
from jax.experimental import pallas as pl
from jax.experimental.pallas import tpu as pltpu
from jax.sharding import PartitionSpec as P

HIGH = lax.Precision.HIGHEST


def shifted(value, axis, by):
    count = lax.axis_size(axis)
    pairs = [(i, i + by) for i in range(count) if 0 <= i + by < count]
    return lax.ppermute(value, axis, pairs)


def carried_in(value, axis, join, neutral, backward):
    count, mine = (lax.axis_size(axis), lax.axis_index(axis))
    pieces = jax.tree.map(lambda part: lax.all_gather(part, axis), value)
    if backward:
        pieces = jax.tree.map(lambda part: part[::-1], pieces)
        mine = count - 1 - mine
    total = jax.tree.map(
        lambda part, zero: jnp.full_like(part, 0) + jnp.asarray(zero, part.dtype), value, neutral
    )

    def turn(position, total):
        longer = join(total, jax.tree.map(lambda part: part[position], pieces))
        return jax.tree.map(lambda new, old: jnp.where(position < mine, new, old), longer, total)

    return lax.fori_loop(0, count - 1, turn, total)


def product(left, right):
    return jnp.dot(left, right, precision=HIGH, preferred_element_type=jnp.float32)


def apply_to(matrix, vectors):
    return product(vectors, matrix.T)


def row_matrix(diag_row, link_row):
    extent = diag_row.shape[0]
    row_ids = lax.broadcasted_iota(jnp.int32, (extent, extent), 0)
    col_ids = lax.broadcasted_iota(jnp.int32, (extent, extent), 1)
    east = col_ids == (row_ids + 1) % extent
    west = row_ids == (col_ids + 1) % extent
    link = jnp.where(east, link_row[:, None], 0.0) + jnp.where(west, link_row[None, :], 0.0)
    return jnp.where(row_ids == col_ids, diag_row[:, None], 0.0) - link


def inverse(matrix):
    factor = jnp.linalg.cholesky(matrix)
    return jax.scipy.linalg.cho_solve((factor, True), jnp.eye(matrix.shape[0], dtype=jnp.float32))


def load_update(factor, upper, lower):
    vector = jax.scipy.linalg.cho_solve((factor, True), (upper[4] + lower[3]).T)
    return (upper[3] - product(upper[1], vector).T, lower[4] - product(lower[1].T, vector).T)


def merge_whole(upper, lower):
    extent = upper[2].shape[0]
    factor = jnp.linalg.cholesky(upper[2] + lower[0])
    solved = jax.scipy.linalg.cho_solve(
        (factor, True), jnp.concatenate([upper[1].T, lower[1]], axis=1)
    )
    first_cols = solved[:, :extent]
    second_cols = solved[:, extent:]
    first_load, second_load = load_update(factor, upper, lower)
    return (
        upper[0] - product(upper[1], first_cols),
        -product(upper[1], second_cols),
        lower[2] - product(lower[1].T, second_cols),
        first_load,
        second_load,
    )


def merge_flagged(upper, lower):
    merged = merge_whole(upper[:5], lower[:5])
    upper_empty = upper[5] > 0.5
    lower_empty = lower[5] > 0.5
    picked = tuple(
        (
            jnp.where(upper_empty, lower_part, jnp.where(lower_empty, upper_part, merged_part))
            for upper_part, lower_part, merged_part in zip(upper[:5], lower[:5], merged)
        )
    )
    return picked + (upper[5] * lower[5],)


def chain_maps(earlier_map, later_map):
    return (
        product(later_map[0], earlier_map[0]),
        later_map[1] + apply_to(later_map[0], earlier_map[1]),
    )


def substitute(value_below, inputs):
    gain, offset = inputs
    value = offset + apply_to(gain, value_below)
    return (value, value)


def latitude_shards(h_cond, v_cond, confidence, teacher, grad_x, grad_y):
    slice_cols = h_cond.shape[1]
    local_rows = h_cond.shape[0]
    hypotheses = teacher.shape[0]
    edge_rows = jnp.concatenate([v_cond[-1][None], v_cond[-1][None] * grad_y[:, -1]], axis=0)
    above = shifted(edge_rows, "strip", 1)
    packed = jnp.concatenate(
        [
            h_cond,
            v_cond,
            confidence,
            above,
            teacher.reshape(hypotheses * local_rows, slice_cols),
            grad_x.reshape(hypotheses * local_rows, slice_cols),
            grad_y.reshape(hypotheses * local_rows, slice_cols),
        ],
        axis=0,
    )
    whole = lax.all_gather(packed, "panel", axis=1, tiled=True)
    extent = whole.shape[1]
    horizontal = whole[:local_rows]
    vertical = whole[local_rows : 2 * local_rows]
    weights = whole[2 * local_rows : 3 * local_rows]
    vertical_edge = whole[3 * local_rows]
    flux_edge = whole[3 * local_rows + 1 : 3 * local_rows + 1 + hypotheses]
    base = 3 * local_rows + 1 + hypotheses
    stride = hypotheses * local_rows
    targets = whole[base : base + stride].reshape(hypotheses, local_rows, extent)
    slope_x = whole[base + stride : base + 2 * stride].reshape(hypotheses, local_rows, extent)
    slope_y = whole[base + 2 * stride : base + 3 * stride].reshape(hypotheses, local_rows, extent)
    vertical_above = jnp.concatenate([vertical_edge[None], vertical[:-1]], axis=0)
    flux = vertical[None] * slope_y
    flux_above = jnp.concatenate([flux_edge[:, None], flux[:, :-1]], axis=1)
    along = horizontal[None] * slope_x
    loads = weights[None] * targets + jnp.roll(along, 1, axis=2) - along + flux_above - flux
    loads = jnp.transpose(loads, (1, 0, 2))
    diagonal = jnp.roll(horizontal, 1, axis=1) + horizontal + vertical_above + vertical + weights
    blocks = jax.vmap(row_matrix)(diagonal, horizontal)
    zeros_mat = jnp.zeros((extent, extent), jnp.float32)
    zeros_vec = jnp.zeros((hypotheses, extent), jnp.float32)
    identity = jnp.eye(extent, dtype=jnp.float32)
    start = (zeros_mat, -jnp.diag(vertical_above[0]), blocks[0], zeros_vec, loads[0])

    def fold_step(segment, inputs):
        matrix_row, coupling, load_row = inputs
        piece = (zeros_mat, -jnp.diag(coupling), matrix_row, zeros_vec, load_row)
        merged = merge_whole(segment, piece)
        return (merged, None)

    segment, _ = lax.scan(fold_step, start, (blocks[1:], vertical_above[1:], loads[1:]))
    filled = segment + (jnp.zeros((), jnp.float32),)
    blank = (zeros_mat, zeros_mat, identity, zeros_vec, zeros_vec, jnp.ones((), jnp.float32))
    prefix = carried_in(filled, "strip", merge_flagged, blank, False)
    prefix_matrix, prefix_load = (prefix[2], prefix[4])

    def eliminate(state, inputs):
        inverse_prev, load_prev, pivot_prev = state
        matrix_row, coupling, load_row, coupling_below = inputs
        pivot = matrix_row - coupling[:, None] * inverse_prev * coupling[None, :]
        carried = load_row + coupling[None, :] * apply_to(inverse_prev, load_prev)
        inverse_now = inverse(pivot)
        return (
            (inverse_now, carried, pivot),
            (inverse_now * coupling_below[None, :], apply_to(inverse_now, carried)),
        )

    final_state, (gains, offsets) = lax.scan(
        eliminate,
        (inverse(prefix_matrix), prefix_load, identity),
        (blocks, vertical_above, loads, vertical),
    )

    def compose(mapping, inputs):
        gain, offset = inputs
        return ((product(gain, mapping[0]), offset + apply_to(gain, mapping[1])), None)

    (reach, moved), _ = lax.scan(compose, (identity, zeros_vec), (gains, offsets), reverse=True)
    beyond = carried_in((reach, moved), "strip", chain_maps, (identity, zeros_vec), True)
    _, solution = lax.scan(substitute, beyond[1], (gains, offsets), reverse=True)
    solution = jnp.transpose(solution, (1, 0, 2))
    return lax.dynamic_slice_in_dim(solution, lax.axis_index("panel") * slice_cols, slice_cols, 2)


SHARED = 2
MESH = pl.DeviceIdType.MESH


def power_of_two(n):
    return n >= 2 and n & (n - 1) == 0


def tall_enough(shape, maps, strips, panels):
    local_rows, cols = shape
    rows, group = local_rows * strips, strips // SHARED
    if not (power_of_two(strips) and panels in (2, 4) and group >= 2 and cols % group == 0):
        return False
    width = cols // group
    lanes = 4 * rows
    return (
        lanes == 128
        and cols <= lanes
        and local_rows >= 3
        and power_of_two(width)
        and width % 8 == 0
        and maps % 8 == 0
        and 2 * maps <= rows
        and local_rows * (maps + 8) <= 3 * rows
        and local_rows <= 8
    )


def lane_block(shape, rows):
    return lax.broadcasted_iota(jnp.int32, shape, 1) // rows


def eliminate(systems, spots, rows, group):
    lanes, pieces = systems[0].shape[1], rows // 8
    shape = (8, lanes)
    row_ids = lax.broadcasted_iota(jnp.int32, shape, 0)
    state = [[m[8 * v : 8 * v + 8] for v in range(pieces)] for m in systems]
    for first in range(0, rows, group):
        columns = [
            [
                [jnp.broadcast_to(p[:, at : at + 1], shape) for p in m]
                for at in range(spot * rows + first, spot * rows + first + group)
            ]
            for m, spot in zip(state, spots)
        ]
        for t in range(group):
            piece, at = divmod(first + t, 8)
            for b in range(len(state)):
                column = columns[b][t]
                scale = 1.0 / column[piece][at : at + 1]
                factors = list(column)
                factors[piece] = jnp.where(row_ids == at, column[piece] - 1.0, column[piece])

                def updated(part):
                    pivot = part[piece][at : at + 1] * scale
                    return [part[v] - factors[v] * pivot for v in range(pieces)]

                state[b] = updated(state[b])
                for u in range(t + 1, group):
                    columns[b][u] = updated(columns[b][u])
    return [jnp.concatenate(m, axis=0) for m in state]


def group_for(count, rows):
    return rows // 2 if count == 1 else rows // 4 if count == 2 else rows // 8


def halves(frame):
    west, middle, east = frame
    return (west, east, middle), (middle, west, east)


def frames_for(count):
    levels, frames = [], [(0, 2, 1)]
    while len(frames) < count:
        levels.append(frames)
        frames = [half for frame in frames for half in halves(frame)]
    return levels[::-1]


def placed(segment, west, east, rows):
    lanes = segment.shape[1]
    block = lane_block(segment.shape, rows)
    at_west = segment if west == 0 else pltpu.roll(segment, west * rows, 1)
    at_east = segment if east == 1 else pltpu.roll(segment, (east - 1) * rows % lanes, 1)
    rest = jnp.where(block == 3, segment, 0.0)
    return jnp.where(block == west, at_west, jnp.where(block == east, at_east, rest))


def thirds(value):
    high = value.astype(jnp.bfloat16).astype(jnp.float32)
    rest = value - high
    middle = rest.astype(jnp.bfloat16).astype(jnp.float32)
    return high, middle, rest - middle


def span_product(left, spot, right, rows):
    block = lane_block(left.shape, rows)
    only = jnp.where(block == spot, left, 0.0)
    everywhere = only
    for step in range(1, 4):
        everywhere = everywhere + pltpu.roll(only, step * rows, 1)
    a, b, c = thirds(everywhere)
    left = jnp.concatenate([jnp.where(block < 3, a, b), jnp.where(block == 0, b, c)[:, : 2 * rows]], axis=1)
    d, e, f = thirds(right)
    right = jnp.concatenate([d, e, f, d, e, d], axis=0)
    return jnp.dot(
        left.astype(jnp.bfloat16), right.astype(jnp.bfloat16), preferred_element_type=jnp.float32
    )


def merge_segments(tops, bottoms, frames, rows):
    spots = [frame[1] for frame in frames]
    pairs = len(frames)
    solved = eliminate(
        [bottoms[2 * i] + tops[2 * i + 1] for i in range(pairs)], spots, rows, group_for(pairs, rows)
    )
    new_tops, new_bottoms = [], []
    for x, spot, west, east in zip(solved, spots, tops[::2], bottoms[1::2]):
        left = jnp.concatenate([west, east], axis=0)
        merged = left - span_product(left, spot, x, rows)
        merged = jnp.where(lane_block(merged.shape, rows) == spot, 0.0, merged)
        new_tops.append(merged[:rows])
        new_bottoms.append(merged[rows:])
    return solved, new_tops, new_bottoms


def merge_tree(tops, bottoms, levels, rows, keep):
    for frames in levels:
        solved, tops, bottoms = merge_segments(tops, bottoms, frames, rows)
        keep(solved)
    return tops, bottoms


def sublanes(value, by):
    rows = value.shape[0]
    if by % rows % 8:
        return pltpu.roll(value, by % rows, 0)
    by = by % rows
    return jnp.concatenate([value[rows - by :], value[: rows - by]], axis=0)


def solve_lines(middles, links, rights, rows):
    span = 1
    state = list(zip(middles, links, rights))
    while span < rows:
        state = [line_step(*s, span) for s in state]
        span *= 2
    return [right / middle for middle, _, right in state]


def line_step(middle, link, right, span):
    inverse_middle = 1.0 / middle
    down = sublanes(link, -span)
    north = link * sublanes(inverse_middle, span)
    south = down * sublanes(inverse_middle, -span)
    return (
        middle - north * link - south * down,
        north * sublanes(link, span),
        right + north * sublanes(right, span) + south * sublanes(right, -span),
    )


def first_merge(fields_ref, frames, rows, maps):
    width = 2 * len(frames)
    lanes = fields_ref.shape[1]
    shape = (rows, lanes)
    block = lane_block(shape, rows)
    lane = lax.broadcasted_iota(jnp.int32, shape, 1)
    row = lax.broadcasted_iota(jnp.int32, shape, 0)
    diagonals = [lane == row + spot * rows for spot in range(3)]
    uppers = [jnp.logical_and(lane == row + spot * rows + 1, block == spot) for spot in range(3)]
    lowers = [jnp.logical_and(lane == row + spot * rows - 1, block == spot) for spot in range(3)]
    load_lane = jnp.logical_and(lane >= 3 * rows, lane < 3 * rows + maps)
    spare = 3 * rows + maps
    east, diagonal, south, north, load = [], [], [], [], []
    for j in range(width):
        f = fields_ref[j * rows : (j + 1) * rows]
        h = jnp.broadcast_to(f[:, spare + 1 : spare + 2], shape)
        v = jnp.broadcast_to(f[:, spare + 2 : spare + 3], shape)
        va = jnp.where(row == 0, 0.0, pltpu.roll(v, 1, 0))
        east.append(h)
        south.append(v)
        north.append(va)
        diagonal.append(jnp.broadcast_to(f[:, spare : spare + 1], shape) + va + h)
        load.append(jnp.where(load_lane, f, 0.0))
    odd = range(1, width, 2)
    solved = solve_lines(
        [diagonal[j] + east[j - 1] for j in odd],
        [north[j] for j in odd],
        [
            load[j]
            - jnp.where(diagonals[frame[0]], east[j - 1], 0.0)
            - jnp.where(diagonals[frame[2]], east[j], 0.0)
            for j, frame in zip(odd, frames)
        ],
        rows,
    )
    tops, bottoms = [], []
    for j, x, (west, _, far) in zip(odd, solved, frames):
        tops.append(
            jnp.where(diagonals[west], diagonal[j - 1], 0.0)
            - jnp.where(uppers[west], south[j - 1], 0.0)
            - jnp.where(lowers[west], north[j - 1], 0.0)
            + load[j - 1]
            + east[j - 1] * x
        )
        bottoms.append(jnp.where(diagonals[far], east[j], 0.0) + east[j] * x)
    return solved, tops, bottoms


def looked_up(x, frame, west, east, rows):
    parts = {frame[0]: west, frame[1]: jnp.zeros_like(west), frame[2]: east}
    right = jnp.concatenate([parts[spot] for spot in range(3)], axis=0)
    return jnp.where(lane_block(x.shape, rows) == 3, x, 0.0) - product(x[:, : 3 * rows], right)


def node_maps(solved, levels, rows, lanes):
    count = 2 * len(levels[0])
    lane = lax.broadcasted_iota(jnp.int32, (rows, lanes), 1)
    row = lax.broadcasted_iota(jnp.int32, (rows, lanes), 0)
    maps = {0: jnp.where(lane == row, -1.0, 0.0), count: jnp.where(lane == row + rows, -1.0, 0.0)}
    position, step = sum(len(frames) for frames in levels), count // 2
    for frames in levels[::-1]:
        position -= len(frames)
        for i, frame in enumerate(frames):
            node = step * (2 * i + 1)
            maps[node] = looked_up(solved(position + i), frame, maps[node - step], maps[node + step], rows)
        step //= 2
    return maps


def compose(maps_in, x, spot, rows):
    x = jnp.where(lane_block(x.shape, rows) == spot, 0.0, x)
    zero = jnp.zeros_like(x)
    right = jnp.concatenate([zero] * spot + [x], axis=0)
    change = product(maps_in[:, : (spot + 1) * rows], right)
    return jnp.where(lane_block(maps_in.shape, rows) == spot, 0.0, maps_in) - change


def flipped(me, mask):
    bit = 1
    peer = me
    while bit <= mask:
        if mask // bit % 2:
            peer = peer + bit * (1 - 2 * (me // bit % 2))
        bit *= 2
    return peer


def exchange(axis, source, target, send, recv, mask):
    me = lax.axis_index(axis)
    peer = flipped(me, mask)
    copy = pltpu.make_async_remote_copy(
        src_ref=source(peer),
        dst_ref=target(me),
        send_sem=send.at[mask - 1],
        recv_sem=recv.at[mask - 1],
        device_id={axis: peer},
        device_id_type=MESH,
    )
    copy.start()
    return copy


def build_messages(h_ref, v_ref, c_ref, t_ref, gx_ref, gy_ref, stack_ref, rows, maps, width):
    local_rows, cols = h_ref.shape
    lanes = stack_ref.shape[1]
    lane = lax.broadcasted_iota(jnp.int32, (maps, lanes), 1)
    wide = lambda a: jnp.concatenate([a, jnp.zeros((a.shape[0], lanes - cols), jnp.float32)], axis=1)
    h, v, c = wide(h_ref[...]), wide(v_ref[...]), wide(c_ref[...])
    flux_above = jnp.zeros((maps, lanes), jnp.float32)
    edge = jnp.zeros((maps, lanes), jnp.float32)
    stride = maps + 8
    blank = jnp.zeros((5, lanes), jnp.float32)
    for r in range(local_rows):
        rows_r = pl.ds(r, maps, stride=local_rows)
        along = h[r : r + 1] * wide(gx_ref[rows_r, :])
        flux = v[r : r + 1] * wide(gy_ref[rows_r, :])
        west = jnp.where(lane == 0, 0.0, pltpu.roll(along, 1, 1))
        load = c[r : r + 1] * wide(t_ref[rows_r, :]) + west - along + flux_above - flux
        small = jnp.concatenate([v[r : r + 1] + c[r : r + 1], h[r : r + 1], v[r : r + 1], blank], axis=0)
        stack_ref[r * stride : r * stride + maps] = load
        stack_ref[r * stride + maps : (r + 1) * stride] = small
        place = cols - width + r
        moved = pltpu.roll(along, (place - cols + 1) % lanes, 1)
        edge = jnp.where(lane == place, moved, edge)
        flux_above = flux
    base = 3 * rows
    if local_rows * stride < base:
        stack_ref[local_rows * stride : base] = jnp.zeros((base - local_rows * stride, lanes), jnp.float32)
    stack_ref[base : base + maps] = flux_above
    stack_ref[base + maps : base + 2 * maps] = edge
    if base + 2 * maps < lanes:
        stack_ref[base + 2 * maps :] = jnp.zeros((lanes - base - 2 * maps, lanes), jnp.float32)
    return stack_ref[...].T


def spread_fields(got_ref, fields_ref, edge_ref, rows, maps, width):
    strips, _, lanes = got_ref.shape
    local_rows = rows // strips
    stride, base = maps + 8, 3 * rows
    shape = (width, lanes)
    lane = lax.broadcasted_iota(jnp.int32, shape, 1)
    load_lane = jnp.logical_and(lane >= base, lane < base + maps)
    for s in range(strips):
        part = got_ref[s]
        for r in range(local_rows):
            moved = pltpu.roll(part, (base - r * stride) % lanes, 1)
            if r == 0 and s > 0:
                moved = moved + jnp.where(load_lane, got_ref[s - 1], 0.0)
            for j in range(0, width, 8):
                fields_ref[pl.ds(j * rows + s * local_rows + r, 8, stride=rows), :] = moved[j : j + 8]
        edge_ref[s * local_rows : (s + 1) * local_rows] = pltpu.roll(part, lanes - maps, 1)[:local_rows]


def pair_merge(pans_ref, side, rows):
    spots = [((0, 1), (1, 2)), ((2, 1), (1, 0))]
    ends = []
    for at in range(2):
        whole = pans_ref[2 * side + at]
        both = jnp.where(side == 0, placed(whole, *spots[0][at], rows), placed(whole, *spots[1][at], rows))
        ends.append((both[:rows], both[rows:]))
    solved, tops, bottoms = merge_segments(*zip(*ends), [(0, 1, 2)], rows)
    return solved[0], (tops[0], bottoms[0])


def solve_kernel(
    h_in, v_in, c_in, t_in, gx_in, gy_in, out_ref,
    h_ref, v_ref, c_ref, t_ref, gx_ref, gy_ref, stack_ref, parts_ref, got_ref, fields_ref, edge_ref,
    local_ref, nodes_ref, near_ref, maps_ref, got_maps_ref, pans_ref, path_ref,
    load_sem, send_in, recv_in, send_near, recv_near, send_maps, recv_maps, send_pan, recv_pan,
    *, rows, maps,
):
    strips, me = lax.axis_size("strip"), lax.axis_index("strip")
    panels, panel = lax.axis_size("panel"), lax.axis_index("panel")
    group, width, lanes = parts_ref.shape
    local_rows = rows // strips
    cols = group * width
    barrier = pltpu.get_barrier_semaphore()
    far_first = list(range(strips - 1, 0, -1))
    for mask in far_first:
        pl.semaphore_signal(barrier, inc=1, device_id={"strip": flipped(me, mask)}, device_id_type=MESH)
    for mask in range(1, panels):
        pl.semaphore_signal(barrier, inc=1, device_id={"panel": flipped(panel, mask)}, device_id_type=MESH)
    pairs = zip((h_in, v_in, c_in, t_in, gx_in, gy_in), (h_ref, v_ref, c_ref, t_ref, gx_ref, gy_ref))
    loads = [pltpu.make_async_copy(a, b, load_sem.at[i]) for i, (a, b) in enumerate(pairs)]
    for copy in loads:
        copy.start()
    for copy in loads:
        copy.wait()
    turned = build_messages(h_ref, v_ref, c_ref, t_ref, gx_ref, gy_ref, stack_ref, rows, maps, width)
    for g in range(group):
        parts_ref[g] = turned[g * width : (g + 1) * width]
    pl.semaphore_wait(barrier, strips - 1 + panels - 1)

    first = [
        exchange("strip", lambda p: parts_ref.at[p % group], lambda m: got_ref.at[m], send_in, recv_in, mask)
        for mask in reversed(far_first)
    ]
    mine = me % group
    got_ref[me] = parts_ref[mine]
    for copy in first:
        copy.wait_recv()
    spread_fields(got_ref, fields_ref, edge_ref, rows, maps, width)
    levels = frames_for(width)
    solved, tops, bottoms = first_merge(fields_ref, levels[0], rows, maps)
    kept = [0]

    def keep(xs):
        for x in xs:
            local_ref[kept[0]] = x
            kept[0] += 1

    keep(solved)
    lane = lax.broadcasted_iota(jnp.int32, (rows, lanes), 1)
    load_lane = jnp.logical_and(lane >= 3 * rows, lane < 3 * rows + maps)
    last_edge = jnp.logical_and(load_lane, mine == group - 1)
    bottoms[-1] = bottoms[-1] + jnp.where(last_edge, edge_ref[...], 0.0)
    (top,), (bottom,) = merge_tree(tops, bottoms, levels[1:], rows, keep)
    near_ref[mine, :rows] = top
    near_ref[mine, rows:] = bottom
    near = [
        exchange("strip", lambda p: near_ref.at[mine], lambda m: near_ref.at[m % group], send_near, recv_near, mask)
        for mask in range(group - 1, 0, -1)
    ]

    columns = node_maps(lambda i: local_ref[i], levels, rows, lanes)
    start = pl.multiple_of((me - mine) * local_rows, group * local_rows)
    for j in range(width):
        nodes_ref[j] = columns[j]
    for j in range(width):
        picked = nodes_ref[j, pl.ds(start, group * local_rows)]
        maps_ref[pl.ds(j, group * local_rows, stride=width), :] = picked
    size = width * local_rows
    spans = lambda p: maps_ref.at[pl.ds(pl.multiple_of(p % group * size, size), size)]
    moved = [
        exchange("strip", spans, lambda m: got_maps_ref.at[m % group], send_maps, recv_maps, mask)
        for mask in range(group - 1, 0, -1)
    ]
    got_maps_ref[mine] = maps_ref[pl.ds(pl.multiple_of(mine * size, size), size)]

    for copy in near:
        copy.wait_recv()
    levels = frames_for(group)
    tops, bottoms = [], []
    for g in range(group):
        half = halves(levels[0][g // 2])[g % 2]
        both = placed(near_ref[g], half[0], half[2], rows)
        tops.append(both[:rows])
        bottoms.append(both[rows:])
    inner = []
    (top,), (bottom,) = merge_tree(tops, bottoms, levels, rows, inner.extend)
    pans_ref[panel, :rows] = top
    pans_ref[panel, rows:] = bottom
    across = [
        exchange("panel", lambda p: pans_ref.at[panel], lambda m: pans_ref.at[m], send_pan, recv_pan, mask)
        for mask in range(1, panels)
    ]
    spots = [(0, 1), (1, 2), (2, 1), (1, 0)] if panels > 2 else [(0, 2), (2, 0)]
    ends = node_maps(lambda i: inner[i], levels, rows, lanes)
    for g in range(group + 1):
        choice = placed(ends[g], *spots[0], rows)
        for p in range(1, panels):
            choice = jnp.where(panel == p, placed(ends[g], *spots[p], rows), choice)
        ends[g] = choice
    for copy in moved:
        copy.wait_recv()
    for g in range(group):
        part = looked_up(got_maps_ref[g], (0, 2, 1), ends[g], ends[g + 1], rows)
        for r in range(local_rows):
            path_ref[r * cols + g * width : r * cols + (g + 1) * width] = part[r * width : (r + 1) * width]
    path = path_ref[...]
    if panels > 2:
        across[0].wait_recv()
        side = panel // 2
        solved, here = pair_merge(pans_ref, side, rows)
        path = compose(path, solved, 1, rows)
        for copy in across[1:]:
            copy.wait_recv()
        _, there = pair_merge(pans_ref, 1 - side, rows)
        ring = [[jnp.where(side == s, h, t) for h, t in zip(here, there)] for s in range(2)]
    else:
        across[0].wait_recv()
        ring = []
        for p in range(panels):
            both = placed(pans_ref[p], *spots[p], rows)
            ring.append((both[:rows], both[rows:]))
    tops, bottoms = zip(*ring)
    middle = eliminate([bottoms[0] + tops[1]], [2], rows, group_for(1, rows))[0]
    around = tops[0] + bottoms[1]
    closing = around - span_product(around, 2, middle, rows)
    final = eliminate([closing], [0], rows, group_for(1, rows))[0]
    turned = compose(path, middle, 2, rows).T
    weight = turned[:rows]
    values = final.T[3 * rows : 3 * rows + maps]
    result = turned[3 * rows : 3 * rows + maps] - product(values, weight)
    for r in range(local_rows):
        out_ref[pl.ds(r, maps, stride=local_rows), :] = result[:, r * cols : (r + 1) * cols]
    for copy in first + near + moved + across:
        copy.wait_send()


def longitude_shards(h_cond, v_cond, confidence, teacher, grad_x, grad_y):
    local_rows, cols = h_cond.shape
    maps = teacher.shape[0]
    strips, panels = lax.axis_size("strip"), lax.axis_size("panel")
    rows, lanes = local_rows * strips, 4 * local_rows * strips
    group = strips // SHARED
    width = cols // group
    f32 = jnp.float32
    dma = pltpu.SemaphoreType.DMA
    flat = (maps * local_rows, cols)
    size = width * local_rows
    values = pl.pallas_call(
        functools.partial(solve_kernel, rows=rows, maps=maps),
        out_shape=pltpu.VMEM(flat, f32),
        in_specs=[pl.BlockSpec(memory_space=pl.ANY)] * 6,
        out_specs=pl.BlockSpec(memory_space=pltpu.VMEM),
        scratch_shapes=[
            pltpu.VMEM((local_rows, cols), f32),
            pltpu.VMEM((local_rows, cols), f32),
            pltpu.VMEM((local_rows, cols), f32),
            pltpu.VMEM(flat, f32),
            pltpu.VMEM(flat, f32),
            pltpu.VMEM(flat, f32),
            pltpu.VMEM((lanes, lanes), f32),
            pltpu.VMEM((group, width, lanes), f32),
            pltpu.VMEM((strips, width, lanes), f32),
            pltpu.VMEM((width * rows, lanes), f32),
            pltpu.VMEM((rows, lanes), f32),
            pltpu.VMEM((width - 1, rows, lanes), f32),
            pltpu.VMEM((width, rows, lanes), f32),
            pltpu.VMEM((group, 2 * rows, lanes), f32),
            pltpu.VMEM((group * size, lanes), f32),
            pltpu.VMEM((group, size, lanes), f32),
            pltpu.VMEM((panels, 2 * rows, lanes), f32),
            pltpu.VMEM((local_rows * cols, lanes), f32),
            dma((6,)),
            dma((strips - 1,)),
            dma((strips - 1,)),
            dma((group - 1,)),
            dma((group - 1,)),
            dma((group - 1,)),
            dma((group - 1,)),
            dma((panels - 1,)),
            dma((panels - 1,)),
        ],
        compiler_params=pltpu.CompilerParams(collective_id=0, has_side_effects=True),
    )(h_cond, v_cond, confidence, *(a.reshape(flat) for a in (teacher, grad_x, grad_y)))
    return values.reshape(maps, local_rows, cols)


def shards(h_cond, v_cond, confidence, teacher, grad_x, grad_y):
    strips, panels = lax.axis_size("strip"), lax.axis_size("panel")
    fits = tall_enough(h_cond.shape, teacher.shape[0], strips, panels)
    body = longitude_shards if fits else latitude_shards
    return body(h_cond, v_cond, confidence, teacher, grad_x, grad_y)


def solution(mesh):
    in_specs = (
        P("strip", "panel"),
        P("strip", "panel"),
        P("strip", "panel"),
        P(None, "strip", "panel"),
        P(None, "strip", "panel"),
        P(None, "strip", "panel"),
    )
    out_specs = P(None, "strip", "panel")
    return jax.shard_map(shards, mesh=mesh, in_specs=in_specs, out_specs=out_specs, check_vma=False)
```

```python
import functools

import jax
import jax.numpy as jnp
from jax import lax
from jax.experimental import pallas as pl
from jax.experimental.pallas import tpu as pltpu
from jax.sharding import PartitionSpec as P

HIGH = lax.Precision.HIGHEST


def shifted(value, axis, by):
    count = lax.axis_size(axis)
    pairs = [(i, i + by) for i in range(count) if 0 <= i + by < count]
    return lax.ppermute(value, axis, pairs)


def carried_in(value, axis, join, neutral, backward):
    count, mine = (lax.axis_size(axis), lax.axis_index(axis))
    pieces = jax.tree.map(lambda part: lax.all_gather(part, axis), value)
    if backward:
        pieces = jax.tree.map(lambda part: part[::-1], pieces)
        mine = count - 1 - mine
    total = jax.tree.map(
        lambda part, zero: jnp.full_like(part, 0) + jnp.asarray(zero, part.dtype), value, neutral
    )

    def turn(position, total):
        longer = join(total, jax.tree.map(lambda part: part[position], pieces))
        return jax.tree.map(lambda new, old: jnp.where(position < mine, new, old), longer, total)

    return lax.fori_loop(0, count - 1, turn, total)


def product(left, right):
    return jnp.dot(left, right, precision=HIGH, preferred_element_type=jnp.float32)


def apply_to(matrix, vectors):
    return product(vectors, matrix.T)


def row_matrix(diag_row, link_row):
    extent = diag_row.shape[0]
    row_ids = lax.broadcasted_iota(jnp.int32, (extent, extent), 0)
    col_ids = lax.broadcasted_iota(jnp.int32, (extent, extent), 1)
    east = col_ids == (row_ids + 1) % extent
    west = row_ids == (col_ids + 1) % extent
    link = jnp.where(east, link_row[:, None], 0.0) + jnp.where(west, link_row[None, :], 0.0)
    return jnp.where(row_ids == col_ids, diag_row[:, None], 0.0) - link


def inverse(matrix):
    factor = jnp.linalg.cholesky(matrix)
    return jax.scipy.linalg.cho_solve((factor, True), jnp.eye(matrix.shape[0], dtype=jnp.float32))


def load_update(factor, upper, lower):
    vector = jax.scipy.linalg.cho_solve((factor, True), (upper[4] + lower[3]).T)
    return (upper[3] - product(upper[1], vector).T, lower[4] - product(lower[1].T, vector).T)


def merge_whole(upper, lower):
    extent = upper[2].shape[0]
    factor = jnp.linalg.cholesky(upper[2] + lower[0])
    solved = jax.scipy.linalg.cho_solve(
        (factor, True), jnp.concatenate([upper[1].T, lower[1]], axis=1)
    )
    first_cols = solved[:, :extent]
    second_cols = solved[:, extent:]
    first_load, second_load = load_update(factor, upper, lower)
    return (
        upper[0] - product(upper[1], first_cols),
        -product(upper[1], second_cols),
        lower[2] - product(lower[1].T, second_cols),
        first_load,
        second_load,
    )


def merge_flagged(upper, lower):
    merged = merge_whole(upper[:5], lower[:5])
    upper_empty = upper[5] > 0.5
    lower_empty = lower[5] > 0.5
    picked = tuple(
        (
            jnp.where(upper_empty, lower_part, jnp.where(lower_empty, upper_part, merged_part))
            for upper_part, lower_part, merged_part in zip(upper[:5], lower[:5], merged)
        )
    )
    return picked + (upper[5] * lower[5],)


def chain_maps(earlier_map, later_map):
    return (
        product(later_map[0], earlier_map[0]),
        later_map[1] + apply_to(later_map[0], earlier_map[1]),
    )


def substitute(value_below, inputs):
    gain, offset = inputs
    value = offset + apply_to(gain, value_below)
    return (value, value)


def latitude_shards(h_cond, v_cond, confidence, teacher, grad_x, grad_y):
    slice_cols = h_cond.shape[1]
    local_rows = h_cond.shape[0]
    hypotheses = teacher.shape[0]
    edge_rows = jnp.concatenate([v_cond[-1][None], v_cond[-1][None] * grad_y[:, -1]], axis=0)
    above = shifted(edge_rows, "strip", 1)
    packed = jnp.concatenate(
        [
            h_cond,
            v_cond,
            confidence,
            above,
            teacher.reshape(hypotheses * local_rows, slice_cols),
            grad_x.reshape(hypotheses * local_rows, slice_cols),
            grad_y.reshape(hypotheses * local_rows, slice_cols),
        ],
        axis=0,
    )
    whole = lax.all_gather(packed, "panel", axis=1, tiled=True)
    extent = whole.shape[1]
    horizontal = whole[:local_rows]
    vertical = whole[local_rows : 2 * local_rows]
    weights = whole[2 * local_rows : 3 * local_rows]
    vertical_edge = whole[3 * local_rows]
    flux_edge = whole[3 * local_rows + 1 : 3 * local_rows + 1 + hypotheses]
    base = 3 * local_rows + 1 + hypotheses
    stride = hypotheses * local_rows
    targets = whole[base : base + stride].reshape(hypotheses, local_rows, extent)
    slope_x = whole[base + stride : base + 2 * stride].reshape(hypotheses, local_rows, extent)
    slope_y = whole[base + 2 * stride : base + 3 * stride].reshape(hypotheses, local_rows, extent)
    vertical_above = jnp.concatenate([vertical_edge[None], vertical[:-1]], axis=0)
    flux = vertical[None] * slope_y
    flux_above = jnp.concatenate([flux_edge[:, None], flux[:, :-1]], axis=1)
    along = horizontal[None] * slope_x
    loads = weights[None] * targets + jnp.roll(along, 1, axis=2) - along + flux_above - flux
    loads = jnp.transpose(loads, (1, 0, 2))
    diagonal = jnp.roll(horizontal, 1, axis=1) + horizontal + vertical_above + vertical + weights
    blocks = jax.vmap(row_matrix)(diagonal, horizontal)
    zeros_mat = jnp.zeros((extent, extent), jnp.float32)
    zeros_vec = jnp.zeros((hypotheses, extent), jnp.float32)
    identity = jnp.eye(extent, dtype=jnp.float32)
    start = (zeros_mat, -jnp.diag(vertical_above[0]), blocks[0], zeros_vec, loads[0])

    def fold_step(segment, inputs):
        matrix_row, coupling, load_row = inputs
        piece = (zeros_mat, -jnp.diag(coupling), matrix_row, zeros_vec, load_row)
        merged = merge_whole(segment, piece)
        return (merged, None)

    segment, _ = lax.scan(fold_step, start, (blocks[1:], vertical_above[1:], loads[1:]))
    filled = segment + (jnp.zeros((), jnp.float32),)
    blank = (zeros_mat, zeros_mat, identity, zeros_vec, zeros_vec, jnp.ones((), jnp.float32))
    prefix = carried_in(filled, "strip", merge_flagged, blank, False)
    prefix_matrix, prefix_load = (prefix[2], prefix[4])

    def eliminate(state, inputs):
        inverse_prev, load_prev, pivot_prev = state
        matrix_row, coupling, load_row, coupling_below = inputs
        pivot = matrix_row - coupling[:, None] * inverse_prev * coupling[None, :]
        carried = load_row + coupling[None, :] * apply_to(inverse_prev, load_prev)
        inverse_now = inverse(pivot)
        return (
            (inverse_now, carried, pivot),
            (inverse_now * coupling_below[None, :], apply_to(inverse_now, carried)),
        )

    final_state, (gains, offsets) = lax.scan(
        eliminate,
        (inverse(prefix_matrix), prefix_load, identity),
        (blocks, vertical_above, loads, vertical),
    )

    def compose(mapping, inputs):
        gain, offset = inputs
        return ((product(gain, mapping[0]), offset + apply_to(gain, mapping[1])), None)

    (reach, moved), _ = lax.scan(compose, (identity, zeros_vec), (gains, offsets), reverse=True)
    beyond = carried_in((reach, moved), "strip", chain_maps, (identity, zeros_vec), True)
    _, solution = lax.scan(substitute, beyond[1], (gains, offsets), reverse=True)
    solution = jnp.transpose(solution, (1, 0, 2))
    return lax.dynamic_slice_in_dim(solution, lax.axis_index("panel") * slice_cols, slice_cols, 2)


SHARED = 2
MESH = pl.DeviceIdType.MESH


def power_of_two(n):
    return n >= 2 and n & (n - 1) == 0


def tall_enough(shape, maps, strips, panels):
    local_rows, cols = shape
    rows, group = local_rows * strips, strips // SHARED
    if not (power_of_two(strips) and panels in (2, 4) and group >= 2 and cols % group == 0):
        return False
    width = cols // group
    lanes = 4 * rows
    return (
        lanes == 128
        and cols <= lanes
        and local_rows >= 3
        and power_of_two(width)
        and width % 8 == 0
        and maps % 8 == 0
        and 2 * maps <= rows
        and local_rows * (maps + 8) <= 3 * rows
        and local_rows <= 8
    )


def lane_block(shape, rows):
    return lax.broadcasted_iota(jnp.int32, shape, 1) // rows


def eliminate(systems, spots, rows, group):
    lanes, pieces = systems[0].shape[1], rows // 8
    shape = (8, lanes)
    row_ids = lax.broadcasted_iota(jnp.int32, shape, 0)
    state = [[m[8 * v : 8 * v + 8] for v in range(pieces)] for m in systems]
    bounds = list(range(0, rows, group)) + [rows]
    if len(bounds) == 3:
        bounds[1] += rows // 16
    for first, after in zip(bounds, bounds[1:]):
        columns = [
            [
                [jnp.broadcast_to(p[:, at : at + 1], shape) for p in m]
                for at in range(spot * rows + first, spot * rows + after)
            ]
            for m, spot in zip(state, spots)
        ]
        for t in range(after - first):
            piece, at = divmod(first + t, 8)
            for b in range(len(state)):
                column = columns[b][t]
                scale = 1.0 / column[piece][at : at + 1]
                factors = list(column)
                factors[piece] = jnp.where(row_ids == at, column[piece] - 1.0, column[piece])

                def updated(part):
                    pivot = part[piece][at : at + 1] * scale
                    return [part[v] - factors[v] * pivot for v in range(pieces)]

                state[b] = updated(state[b])
                for u in range(t + 1, after - first):
                    columns[b][u] = updated(columns[b][u])
    return [jnp.concatenate(m, axis=0) for m in state]


def group_for(count, rows):
    return rows // 2 if count == 1 else rows // 4 if count == 2 else rows // 8


def halves(frame):
    west, middle, east = frame
    return (west, east, middle), (middle, west, east)


def frames_for(count):
    levels, frames = [], [(0, 2, 1)]
    while len(frames) < count:
        levels.append(frames)
        frames = [half for frame in frames for half in halves(frame)]
    return levels[::-1]


def placed(segment, west, east, rows):
    lanes = segment.shape[1]
    block = lane_block(segment.shape, rows)
    at_west = segment if west == 0 else pltpu.roll(segment, west * rows, 1)
    at_east = segment if east == 1 else pltpu.roll(segment, (east - 1) * rows % lanes, 1)
    rest = jnp.where(block == 3, segment, 0.0)
    return jnp.where(block == west, at_west, jnp.where(block == east, at_east, rest))


def thirds(value):
    high = value.astype(jnp.bfloat16).astype(jnp.float32)
    rest = value - high
    middle = rest.astype(jnp.bfloat16).astype(jnp.float32)
    return high, middle, rest - middle


def span_product(left, spot, right, rows):
    block = lane_block(left.shape, rows)
    only = jnp.where(block == spot, left, 0.0)
    everywhere = only
    for step in range(1, 4):
        everywhere = everywhere + pltpu.roll(only, step * rows, 1)
    a, b, c = thirds(everywhere)
    left = jnp.concatenate([jnp.where(block < 3, a, b), jnp.where(block == 0, b, c)[:, : 2 * rows]], axis=1)
    d, e, f = thirds(right)
    right = jnp.concatenate([d, e, f, d, e, d], axis=0)
    return jnp.dot(
        left.astype(jnp.bfloat16), right.astype(jnp.bfloat16), preferred_element_type=jnp.float32
    )


def merge_segments(tops, bottoms, frames, rows):
    spots = [frame[1] for frame in frames]
    pairs = len(frames)
    solved = eliminate(
        [bottoms[2 * i] + tops[2 * i + 1] for i in range(pairs)], spots, rows, group_for(pairs, rows)
    )
    new_tops, new_bottoms = [], []
    for x, spot, west, east in zip(solved, spots, tops[::2], bottoms[1::2]):
        left = jnp.concatenate([west, east], axis=0)
        merged = left - span_product(left, spot, x, rows)
        merged = jnp.where(lane_block(merged.shape, rows) == spot, 0.0, merged)
        new_tops.append(merged[:rows])
        new_bottoms.append(merged[rows:])
    return solved, new_tops, new_bottoms


def merge_tree(tops, bottoms, levels, rows, keep):
    for frames in levels:
        solved, tops, bottoms = merge_segments(tops, bottoms, frames, rows)
        keep(solved)
    return tops, bottoms


def sublanes(value, by):
    rows = value.shape[0]
    if by % rows % 8:
        return pltpu.roll(value, by % rows, 0)
    by = by % rows
    return jnp.concatenate([value[rows - by :], value[: rows - by]], axis=0)


def solve_lines(middles, links, rights, rows):
    span = 1
    state = list(zip(middles, links, rights))
    while span < rows:
        state = [line_step(*s, span) for s in state]
        span *= 2
    return [right / middle for middle, _, right in state]


def line_step(middle, link, right, span):
    inverse_middle = 1.0 / middle
    down = sublanes(link, -span)
    north = link * sublanes(inverse_middle, span)
    south = down * sublanes(inverse_middle, -span)
    return (
        middle - north * link - south * down,
        north * sublanes(link, span),
        right + north * sublanes(right, span) + south * sublanes(right, -span),
    )


def first_merge(fields_ref, frames, rows, maps):
    width = 2 * len(frames)
    lanes = fields_ref.shape[1]
    shape = (rows, lanes)
    block = lane_block(shape, rows)
    lane = lax.broadcasted_iota(jnp.int32, shape, 1)
    row = lax.broadcasted_iota(jnp.int32, shape, 0)
    diagonals = [lane == row + spot * rows for spot in range(3)]
    uppers = [jnp.logical_and(lane == row + spot * rows + 1, block == spot) for spot in range(3)]
    lowers = [jnp.logical_and(lane == row + spot * rows - 1, block == spot) for spot in range(3)]
    load_lane = jnp.logical_and(lane >= 3 * rows, lane < 3 * rows + maps)
    spare = 3 * rows + maps
    east, diagonal, south, north, load = [], [], [], [], []
    for j in range(width):
        f = fields_ref[j * rows : (j + 1) * rows]
        h = jnp.broadcast_to(f[:, spare + 1 : spare + 2], shape)
        v = jnp.broadcast_to(f[:, spare + 2 : spare + 3], shape)
        va = jnp.where(row == 0, 0.0, pltpu.roll(v, 1, 0))
        east.append(h)
        south.append(v)
        north.append(va)
        diagonal.append(jnp.broadcast_to(f[:, spare : spare + 1], shape) + va + h)
        load.append(jnp.where(load_lane, f, 0.0))
    odd = range(1, width, 2)
    solved = solve_lines(
        [diagonal[j] + east[j - 1] for j in odd],
        [north[j] for j in odd],
        [
            load[j]
            - jnp.where(diagonals[frame[0]], east[j - 1], 0.0)
            - jnp.where(diagonals[frame[2]], east[j], 0.0)
            for j, frame in zip(odd, frames)
        ],
        rows,
    )
    tops, bottoms = [], []
    for j, x, (west, _, far) in zip(odd, solved, frames):
        tops.append(
            jnp.where(diagonals[west], diagonal[j - 1], 0.0)
            - jnp.where(uppers[west], south[j - 1], 0.0)
            - jnp.where(lowers[west], north[j - 1], 0.0)
            + load[j - 1]
            + east[j - 1] * x
        )
        bottoms.append(jnp.where(diagonals[far], east[j], 0.0) + east[j] * x)
    return solved, tops, bottoms


def looked_up(x, frame, west, east, rows):
    parts = {frame[0]: west, frame[1]: jnp.zeros_like(west), frame[2]: east}
    right = jnp.concatenate([parts[spot] for spot in range(3)], axis=0)
    return jnp.where(lane_block(x.shape, rows) == 3, x, 0.0) - product(x[:, : 3 * rows], right)


def node_maps(solved, levels, rows, lanes):
    count = 2 * len(levels[0])
    lane = lax.broadcasted_iota(jnp.int32, (rows, lanes), 1)
    row = lax.broadcasted_iota(jnp.int32, (rows, lanes), 0)
    maps = {0: jnp.where(lane == row, -1.0, 0.0), count: jnp.where(lane == row + rows, -1.0, 0.0)}
    position, step = sum(len(frames) for frames in levels), count // 2
    for frames in levels[::-1]:
        position -= len(frames)
        for i, frame in enumerate(frames):
            node = step * (2 * i + 1)
            maps[node] = looked_up(solved(position + i), frame, maps[node - step], maps[node + step], rows)
        step //= 2
    return maps


def compose(maps_in, x, spot, rows):
    x = jnp.where(lane_block(x.shape, rows) == spot, 0.0, x)
    zero = jnp.zeros_like(x)
    right = jnp.concatenate([zero] * spot + [x], axis=0)
    change = product(maps_in[:, : (spot + 1) * rows], right)
    return jnp.where(lane_block(maps_in.shape, rows) == spot, 0.0, maps_in) - change


def flipped(me, mask):
    bit = 1
    peer = me
    while bit <= mask:
        if mask // bit % 2:
            peer = peer + bit * (1 - 2 * (me // bit % 2))
        bit *= 2
    return peer


def exchange(axis, source, target, send, recv, mask):
    me = lax.axis_index(axis)
    peer = flipped(me, mask)
    copy = pltpu.make_async_remote_copy(
        src_ref=source(peer),
        dst_ref=target(me),
        send_sem=send.at[mask - 1],
        recv_sem=recv.at[mask - 1],
        device_id={axis: peer},
        device_id_type=MESH,
    )
    copy.start()
    return copy


def build_messages(h_ref, v_ref, c_ref, t_ref, gx_ref, gy_ref, stack_ref, rows, maps, width):
    local_rows, cols = h_ref.shape
    lanes = stack_ref.shape[1]
    lane = lax.broadcasted_iota(jnp.int32, (maps, lanes), 1)
    wide = lambda a: jnp.concatenate([a, jnp.zeros((a.shape[0], lanes - cols), jnp.float32)], axis=1)
    h, v, c = wide(h_ref[...]), wide(v_ref[...]), wide(c_ref[...])
    flux_above = jnp.zeros((maps, lanes), jnp.float32)
    edge = jnp.zeros((maps, lanes), jnp.float32)
    stride = maps + 8
    blank = jnp.zeros((5, lanes), jnp.float32)
    for r in range(local_rows):
        rows_r = pl.ds(r, maps, stride=local_rows)
        along = h[r : r + 1] * wide(gx_ref[rows_r, :])
        flux = v[r : r + 1] * wide(gy_ref[rows_r, :])
        west = jnp.where(lane == 0, 0.0, pltpu.roll(along, 1, 1))
        load = c[r : r + 1] * wide(t_ref[rows_r, :]) + west - along + flux_above - flux
        small = jnp.concatenate([v[r : r + 1] + c[r : r + 1], h[r : r + 1], v[r : r + 1], blank], axis=0)
        stack_ref[r * stride : r * stride + maps] = load
        stack_ref[r * stride + maps : (r + 1) * stride] = small
        place = cols - width + r
        moved = pltpu.roll(along, (place - cols + 1) % lanes, 1)
        edge = jnp.where(lane == place, moved, edge)
        flux_above = flux
    base = 3 * rows
    if local_rows * stride < base:
        stack_ref[local_rows * stride : base] = jnp.zeros((base - local_rows * stride, lanes), jnp.float32)
    stack_ref[base : base + maps] = flux_above
    stack_ref[base + maps : base + 2 * maps] = edge
    if base + 2 * maps < lanes:
        stack_ref[base + 2 * maps :] = jnp.zeros((lanes - base - 2 * maps, lanes), jnp.float32)
    return stack_ref[...].T


def spread_fields(got_ref, fields_ref, edge_ref, rows, maps, width):
    strips, _, lanes = got_ref.shape
    local_rows = rows // strips
    stride, base = maps + 8, 3 * rows
    shape = (width, lanes)
    lane = lax.broadcasted_iota(jnp.int32, shape, 1)
    load_lane = jnp.logical_and(lane >= base, lane < base + maps)
    for s in range(strips):
        part = got_ref[s]
        for r in range(local_rows):
            moved = pltpu.roll(part, (base - r * stride) % lanes, 1)
            if r == 0 and s > 0:
                moved = moved + jnp.where(load_lane, got_ref[s - 1], 0.0)
            for j in range(0, width, 8):
                fields_ref[pl.ds(j * rows + s * local_rows + r, 8, stride=rows), :] = moved[j : j + 8]
        edge_ref[s * local_rows : (s + 1) * local_rows] = pltpu.roll(part, lanes - maps, 1)[:local_rows]


def pair_merge(pans_ref, side, rows):
    spots = [((0, 1), (1, 2)), ((2, 1), (1, 0))]
    ends = []
    for at in range(2):
        whole = pans_ref[2 * side + at]
        both = jnp.where(side == 0, placed(whole, *spots[0][at], rows), placed(whole, *spots[1][at], rows))
        ends.append((both[:rows], both[rows:]))
    solved, tops, bottoms = merge_segments(*zip(*ends), [(0, 1, 2)], rows)
    return solved[0], (tops[0], bottoms[0])


def solve_kernel(
    h_in, v_in, c_in, t_in, gx_in, gy_in, out_ref,
    h_ref, v_ref, c_ref, t_ref, gx_ref, gy_ref, stack_ref, parts_ref, got_ref, fields_ref, edge_ref,
    local_ref, nodes_ref, near_ref, maps_ref, got_maps_ref, pans_ref, path_ref,
    load_sem, send_in, recv_in, send_near, recv_near, send_maps, recv_maps, send_pan, recv_pan,
    *, rows, maps,
):
    strips, me = lax.axis_size("strip"), lax.axis_index("strip")
    panels, panel = lax.axis_size("panel"), lax.axis_index("panel")
    group, width, lanes = parts_ref.shape
    local_rows = rows // strips
    cols = group * width
    barrier = pltpu.get_barrier_semaphore()
    far_first = list(range(strips - 1, 0, -1))
    for mask in far_first:
        pl.semaphore_signal(barrier, inc=1, device_id={"strip": flipped(me, mask)}, device_id_type=MESH)
    for mask in range(1, panels):
        pl.semaphore_signal(barrier, inc=1, device_id={"panel": flipped(panel, mask)}, device_id_type=MESH)
    pairs = zip((h_in, v_in, c_in, t_in, gx_in, gy_in), (h_ref, v_ref, c_ref, t_ref, gx_ref, gy_ref))
    loads = [pltpu.make_async_copy(a, b, load_sem.at[i]) for i, (a, b) in enumerate(pairs)]
    for copy in loads:
        copy.start()
    for copy in loads:
        copy.wait()
    turned = build_messages(h_ref, v_ref, c_ref, t_ref, gx_ref, gy_ref, stack_ref, rows, maps, width)
    for g in range(group):
        parts_ref[g] = turned[g * width : (g + 1) * width]
    pl.semaphore_wait(barrier, strips - 1 + panels - 1)

    first = [
        exchange("strip", lambda p: parts_ref.at[p % group], lambda m: got_ref.at[m], send_in, recv_in, mask)
        for mask in reversed(far_first)
    ]
    mine = me % group
    got_ref[me] = parts_ref[mine]
    for copy in first:
        copy.wait_recv()
    spread_fields(got_ref, fields_ref, edge_ref, rows, maps, width)
    levels = frames_for(width)
    solved, tops, bottoms = first_merge(fields_ref, levels[0], rows, maps)
    kept = [0]

    def keep(xs):
        for x in xs:
            local_ref[kept[0]] = x
            kept[0] += 1

    keep(solved)
    lane = lax.broadcasted_iota(jnp.int32, (rows, lanes), 1)
    load_lane = jnp.logical_and(lane >= 3 * rows, lane < 3 * rows + maps)
    last_edge = jnp.logical_and(load_lane, mine == group - 1)
    bottoms[-1] = bottoms[-1] + jnp.where(last_edge, edge_ref[...], 0.0)
    (top,), (bottom,) = merge_tree(tops, bottoms, levels[1:], rows, keep)
    near_ref[mine, :rows] = top
    near_ref[mine, rows:] = bottom
    near = [
        exchange("strip", lambda p: near_ref.at[mine], lambda m: near_ref.at[m % group], send_near, recv_near, mask)
        for mask in range(group - 1, 0, -1)
    ]

    columns = node_maps(lambda i: local_ref[i], levels, rows, lanes)
    start = pl.multiple_of((me - mine) * local_rows, group * local_rows)
    for j in range(width):
        nodes_ref[j] = columns[j]
    for j in range(width):
        picked = nodes_ref[j, pl.ds(start, group * local_rows)]
        maps_ref[pl.ds(j, group * local_rows, stride=width), :] = picked
    size = width * local_rows
    spans = lambda p: maps_ref.at[pl.ds(pl.multiple_of(p % group * size, size), size)]
    moved = [
        exchange("strip", spans, lambda m: got_maps_ref.at[m % group], send_maps, recv_maps, mask)
        for mask in range(group - 1, 0, -1)
    ]
    got_maps_ref[mine] = maps_ref[pl.ds(pl.multiple_of(mine * size, size), size)]

    for copy in near:
        copy.wait_recv()
    levels = frames_for(group)
    tops, bottoms = [], []
    for g in range(group):
        half = halves(levels[0][g // 2])[g % 2]
        both = placed(near_ref[g], half[0], half[2], rows)
        tops.append(both[:rows])
        bottoms.append(both[rows:])
    inner = []
    (top,), (bottom,) = merge_tree(tops, bottoms, levels, rows, inner.extend)
    pans_ref[panel, :rows] = top
    pans_ref[panel, rows:] = bottom
    across = [
        exchange("panel", lambda p: pans_ref.at[panel], lambda m: pans_ref.at[m], send_pan, recv_pan, mask)
        for mask in range(1, panels)
    ]
    spots = [(0, 1), (1, 2), (2, 1), (1, 0)] if panels > 2 else [(0, 2), (2, 0)]
    ends = node_maps(lambda i: inner[i], levels, rows, lanes)
    for g in range(group + 1):
        choice = placed(ends[g], *spots[0], rows)
        for p in range(1, panels):
            choice = jnp.where(panel == p, placed(ends[g], *spots[p], rows), choice)
        ends[g] = choice
    for copy in moved:
        copy.wait_recv()
    for g in range(group):
        part = looked_up(got_maps_ref[g], (0, 2, 1), ends[g], ends[g + 1], rows)
        for r in range(local_rows):
            path_ref[r * cols + g * width : r * cols + (g + 1) * width] = part[r * width : (r + 1) * width]
    path = path_ref[...]
    if panels > 2:
        across[0].wait_recv()
        side = panel // 2
        solved, here = pair_merge(pans_ref, side, rows)
        path = compose(path, solved, 1, rows)
        for copy in across[1:]:
            copy.wait_recv()
        _, there = pair_merge(pans_ref, 1 - side, rows)
        ring = [[jnp.where(side == s, h, t) for h, t in zip(here, there)] for s in range(2)]
    else:
        across[0].wait_recv()
        ring = []
        for p in range(panels):
            both = placed(pans_ref[p], *spots[p], rows)
            ring.append((both[:rows], both[rows:]))
    tops, bottoms = zip(*ring)
    middle = eliminate([bottoms[0] + tops[1]], [2], rows, group_for(1, rows))[0]
    around = tops[0] + bottoms[1]
    closing = around - span_product(around, 2, middle, rows)
    final = eliminate([closing], [0], rows, group_for(1, rows))[0]
    turned = compose(path, middle, 2, rows).T
    weight = turned[:rows]
    values = final.T[3 * rows : 3 * rows + maps]
    result = turned[3 * rows : 3 * rows + maps] - product(values, weight)
    for r in range(local_rows):
        out_ref[pl.ds(r, maps, stride=local_rows), :] = result[:, r * cols : (r + 1) * cols]
    for copy in first + near + moved + across:
        copy.wait_send()


def longitude_shards(h_cond, v_cond, confidence, teacher, grad_x, grad_y):
    local_rows, cols = h_cond.shape
    maps = teacher.shape[0]
    strips, panels = lax.axis_size("strip"), lax.axis_size("panel")
    rows, lanes = local_rows * strips, 4 * local_rows * strips
    group = strips // SHARED
    width = cols // group
    f32 = jnp.float32
    dma = pltpu.SemaphoreType.DMA
    flat = (maps * local_rows, cols)
    size = width * local_rows
    values = pl.pallas_call(
        functools.partial(solve_kernel, rows=rows, maps=maps),
        out_shape=pltpu.VMEM(flat, f32),
        in_specs=[pl.BlockSpec(memory_space=pl.ANY)] * 6,
        out_specs=pl.BlockSpec(memory_space=pltpu.VMEM),
        scratch_shapes=[
            pltpu.VMEM((local_rows, cols), f32),
            pltpu.VMEM((local_rows, cols), f32),
            pltpu.VMEM((local_rows, cols), f32),
            pltpu.VMEM(flat, f32),
            pltpu.VMEM(flat, f32),
            pltpu.VMEM(flat, f32),
            pltpu.VMEM((lanes, lanes), f32),
            pltpu.VMEM((group, width, lanes), f32),
            pltpu.VMEM((strips, width, lanes), f32),
            pltpu.VMEM((width * rows, lanes), f32),
            pltpu.VMEM((rows, lanes), f32),
            pltpu.VMEM((width - 1, rows, lanes), f32),
            pltpu.VMEM((width, rows, lanes), f32),
            pltpu.VMEM((group, 2 * rows, lanes), f32),
            pltpu.VMEM((group * size, lanes), f32),
            pltpu.VMEM((group, size, lanes), f32),
            pltpu.VMEM((panels, 2 * rows, lanes), f32),
            pltpu.VMEM((local_rows * cols, lanes), f32),
            dma((6,)),
            dma((strips - 1,)),
            dma((strips - 1,)),
            dma((group - 1,)),
            dma((group - 1,)),
            dma((group - 1,)),
            dma((group - 1,)),
            dma((panels - 1,)),
            dma((panels - 1,)),
        ],
        compiler_params=pltpu.CompilerParams(collective_id=0, has_side_effects=True),
    )(h_cond, v_cond, confidence, *(a.reshape(flat) for a in (teacher, grad_x, grad_y)))
    return values.reshape(maps, local_rows, cols)


def shards(h_cond, v_cond, confidence, teacher, grad_x, grad_y):
    strips, panels = lax.axis_size("strip"), lax.axis_size("panel")
    fits = tall_enough(h_cond.shape, teacher.shape[0], strips, panels)
    body = longitude_shards if fits else latitude_shards
    return body(h_cond, v_cond, confidence, teacher, grad_x, grad_y)


def solution(mesh):
    in_specs = (
        P("strip", "panel"),
        P("strip", "panel"),
        P("strip", "panel"),
        P(None, "strip", "panel"),
        P(None, "strip", "panel"),
        P(None, "strip", "panel"),
    )
    out_specs = P(None, "strip", "panel")
    return jax.shard_map(shards, mesh=mesh, in_specs=in_specs, out_specs=out_specs, check_vma=False)
```
